256 devices in a mesh: dp: 8 (over x, core), expert: 32 (over z, y).
Axes of the slice: x: 4, y: 4, z: 8, core: 2. Of those that a mesh axis runs over, the one named last changes fastest.
Arguments:
- tokens: bfloat16 [12288, 2048], P(('dp', 'expert')), may hold values from -6 to 6
- expert_ids: int32 [12288, 8], P(('dp', 'expert')), may hold values from 0 to 31, all different within a row; in each aligned block of 48 rows (0 to 47, 48 to 95, ...) at most 16 rows name the same one
- gate_probs: float32 [12288, 8], P(('dp', 'expert')), may hold values from 0.05 to 0.5
- out_cot: bfloat16 [12288, 2048], P(('dp', 'expert')), may hold values from -1.5 to 1.5
- w_gate: bfloat16 [32, 2048, 768], P('expert'), may hold values from -0.125 to 0.125
- w_up: bfloat16 [32, 2048, 768], P('expert'), may hold values from -0.125 to 0.125
- w_down: bfloat16 [32, 768, 2048], P('expert'), may hold values from -0.21875 to 0.21875
Outputs:
- layer_out: bfloat16 [12288, 2048], P(('dp', 'expert'))
- input_grad: bfloat16 [12288, 2048], P(('dp', 'expert'))
- gate_wgrad: float32 [32, 2048, 768], P('expert', 'dp')
- up_wgrad: float32 [32, 2048, 768], P('expert', 'dp')
- down_wgrad: float32 [32, 768, 2048], P('expert', 'dp')
The draws below stay inside these ranges and needn't reach their ends.
Inputs may be any that keep to these rules, and one draw needn't show every extreme that they name: `expert_ids`: each token names 8 different experts. Among the 48 tokens of one device, at most 16 name the same expert, and in every draw some expert is named by exactly 16 tokens of some device.
All inputs are finite; a program needn't handle non-finite values.
Results may differ from the reference program's by a relative error of at most 0.012.
Values may be sent and summed in bfloat16 or wider, within the bound.
A program may use at most 128 MiB of HBM per device.

```python
import math
import jax
import jax.numpy as jnp
import numpy as np
from jax import lax

D = 2048
FF = 768
TOP = 8
TOK_DEV = 48
EXPERTS = 32
CAP = 16
TOKENS = 12288
N_DP = 8
N_EXPERT = 32


def block_scale(own_key, extent, cuts, smallest, high):
    def one(axis_at, parts):
        steps = jax.random.uniform(jax.random.fold_in(jax.random.fold_in(own_key, 6), axis_at), (parts,), jnp.float32, smallest / len(cuts), high / len(cuts))
        return jnp.repeat(jnp.exp(steps), extent[axis_at] // parts).reshape((-1,) + (1,) * (len(extent) - axis_at - 1))

    level = one(*cuts[0])
    for cut in cuts[1:]:
        level = level * one(*cut)
    return level


def assign_block(stream_key, own, number, rows, amount, top, bound, lean):
    ranking = jax.random.permutation(stream_key, amount)
    packed, ordinary = load_shares(amount, rows * top, bound, lean, True), load_shares(amount, rows * top, bound, lean, False)
    places = jnp.arange(amount)

    def named(lengths, rotation):
        used = int((lengths > 0).sum())
        fixed = max(1, used // 4)
        moved = fixed + (places - fixed + rotation * (used - fixed)) % max(1, amount - fixed)
        return jnp.zeros((amount,), jnp.int32).at[ranking[jnp.where(places < fixed, places, moved)]].set(jnp.asarray(lengths, jnp.int32))

    lengths = jnp.where(number % 4 == 0, named(packed, number // 4), named(ordinary, number - number // 4 - 1))
    mixed = jax.random.permutation(jax.random.fold_in(own, 3), amount)
    source_of, taker = mixed[0:amount // 2 * 2:2], mixed[1:amount // 2 * 2:2]
    slack = jnp.minimum(lengths[source_of] - 1, bound - lengths[taker]) // 2
    slack = jnp.where((source_of == ranking[0]) | (taker == ranking[0]) | (lengths[taker] == 0), 0, jnp.maximum(slack, 0))
    moved = jax.random.randint(jax.random.fold_in(own, 4), (amount // 2,), 0, 1 << 20) % (slack + 1)
    lengths = lengths.at[source_of].add(-moved).at[taker].add(moved)
    labels = jnp.searchsorted(jnp.cumsum(lengths), jnp.arange(rows * top), side="right").astype(jnp.int32)
    grid = labels.reshape(top, rows).T
    grid = grid[jax.random.permutation(jax.random.fold_in(own, 1), rows)]
    rotation = jax.random.randint(jax.random.fold_in(own, 2), (rows, 1), 0, top)
    return jnp.take_along_axis(grid, (jnp.arange(top)[None, :] + rotation) % top, axis=1)


def load_shares(amount, total, bound, lean, full):
    weights = [(1 << 20) // math.isqrt(rank ** lean) + 1 for rank in range(1, amount + 1)]
    largest = bound if full else min(bound, max(-(-total // amount), total * weights[0] // sum(weights)))
    least = 1 if total - largest >= amount - 1 else 0
    given, rest = [largest] + [least] * (amount - 1), total - largest - least * (amount - 1)
    while rest > 0:
        free = [i for i in range(1, amount) if given[i] < largest] or [i for i in range(1, amount) if given[i] < bound]
        pool, remaining = sum([weights[i] for i in free]), rest
        for i in free:
            extra = min(bound - given[i], max(1, remaining * weights[i] // pool), rest)
            given[i] = given[i] + extra
            rest = rest - extra
    return np.array(given)


def noise(key, dims, deviation, bound, pieces=(), kind=jnp.bfloat16):
    loudness = block_scale(key, dims, pieces, -0.22, 0.18) if pieces else 1.0
    drawn = jax.random.normal(key, dims, jnp.float32) * deviation * loudness
    return jnp.minimum(jnp.maximum(drawn, -bound), bound).astype(kind)


def setup_inputs(seed: int = 0) -> dict:
    keys = jax.random.split(jax.random.key(seed), 8)
    tokens = noise(keys[0], (TOKENS, D), 1.0, 6.0, ((0, 256),))
    expert_ids_keys = jax.random.split(jax.random.fold_in(keys[1], 1), TOKENS // TOK_DEV)
    expert_ids_turns = jax.random.permutation(jax.random.fold_in(keys[1], 3), TOKENS // TOK_DEV)
    expert_ids = jax.vmap(lambda own, number: assign_block(jax.random.fold_in(keys[1], 2), own, number, TOK_DEV, EXPERTS, TOP, CAP, 2))(expert_ids_keys, expert_ids_turns).reshape((TOKENS, TOP))
    gate_probs = jnp.clip(jnp.exp(math.log(0.5) - 2.3025851 * jax.random.uniform(keys[2], (TOKENS, TOP), jnp.float32) ** block_scale(keys[2], (TOKENS, TOP), ((0, 256),), -0.2, 0.2)), 0.05, 0.5)
    out_cot = noise(keys[3], (TOKENS, D), 0.25, 1.5, ((0, 256),))
    w_gate = noise(keys[4], (EXPERTS, D, FF), D ** -0.5, 0.125, ((0, 32),))
    w_up = noise(keys[5], (EXPERTS, D, FF), D ** -0.5, 0.125, ((0, 32),))
    w_down = noise(keys[6], (EXPERTS, FF, D), FF ** -0.5, 0.21875, ((0, 32),))
    return {"tokens": tokens, "expert_ids": expert_ids, "gate_probs": gate_probs, "out_cot": out_cot, "w_gate": w_gate, "w_up": w_up, "w_down": w_down}


def reference(tokens, expert_ids, gate_probs, out_cot, w_gate, w_up, w_down):
    group_tokens = TOK_DEV * N_EXPERT
    window = N_EXPERT * CAP

    def one_group(wgrads, group):
        begin = (group * group_tokens).astype(jnp.int32)
        own_tokens = lax.dynamic_slice_in_dim(tokens, begin, group_tokens, 0)
        own_cot = lax.dynamic_slice_in_dim(out_cot, begin, group_tokens, 0)
        flat_ids = lax.dynamic_slice_in_dim(expert_ids, begin, group_tokens, 0).reshape(-1).astype(jnp.int32)
        flat_probs = lax.dynamic_slice_in_dim(gate_probs, begin, group_tokens, 0).reshape(-1)
        order = jnp.argsort(flat_ids, stable=True).astype(jnp.int32)
        totals = jnp.sum((flat_ids[:, None] == jnp.arange(EXPERTS, dtype=jnp.int32)[None, :]).astype(jnp.int32), axis=0)
        starts = (jnp.cumsum(totals) - totals).astype(jnp.int32)
        padded = jnp.concatenate([order, jnp.zeros((window,), jnp.int32)])

        def one_expert(carry, expert):
            out_total, grad_total = carry
            index = lax.dynamic_slice(padded, (starts[expert],), (window,))
            live = jnp.arange(window, dtype=jnp.int32) < totals[expert]
            owner = (index // TOP).astype(jnp.int32)
            probs = jnp.where(live, flat_probs[index], 0.0)
            rows = jnp.where(live[:, None], own_tokens[owner], 0).astype(tokens.dtype)
            gate_mat = w_gate[expert]
            up_mat = w_up[expert]
            down_mat = w_down[expert]
            gate_pre = jnp.dot(rows, gate_mat, preferred_element_type=jnp.float32)
            up_pre = jnp.dot(rows, up_mat, preferred_element_type=jnp.float32)
            sigma = jax.nn.sigmoid(gate_pre)
            hidden = (gate_pre * sigma * up_pre).astype(jnp.bfloat16)
            expert_out = jnp.dot(hidden, down_mat, preferred_element_type=jnp.float32).astype(jnp.bfloat16)
            out_total = out_total.at[owner].add(probs[:, None] * expert_out.astype(jnp.float32))
            out_grad = (probs[:, None] * own_cot[owner].astype(jnp.float32)).astype(jnp.bfloat16)
            hidden_grad = jnp.dot(out_grad, down_mat.T, preferred_element_type=jnp.float32)
            gate_grad = (hidden_grad * up_pre * sigma * (1.0 + gate_pre * (1.0 - sigma))).astype(jnp.bfloat16)
            up_grad = (hidden_grad * gate_pre * sigma).astype(jnp.bfloat16)
            row_grad = (jnp.dot(gate_grad, gate_mat.T, preferred_element_type=jnp.float32)
                        + jnp.dot(up_grad, up_mat.T, preferred_element_type=jnp.float32)).astype(jnp.bfloat16)
            grad_total = grad_total.at[owner].add(row_grad.astype(jnp.float32))
            gate_w = jnp.dot(rows.T, gate_grad, preferred_element_type=jnp.float32).astype(jnp.bfloat16)
            up_w = jnp.dot(rows.T, up_grad, preferred_element_type=jnp.float32).astype(jnp.bfloat16)
            down_w = jnp.dot(hidden.T, out_grad, preferred_element_type=jnp.float32).astype(jnp.bfloat16)
            return (out_total, grad_total), (gate_w, up_w, down_w)

        start = (jnp.zeros((group_tokens, D), jnp.float32), jnp.zeros((group_tokens, D), jnp.float32))
        (out_total, grad_total), (gate_w, up_w, down_w) = lax.scan(
            one_expert, start, jnp.arange(EXPERTS, dtype=jnp.int32))
        gate_sum, up_sum, down_sum = wgrads
        wgrads = (gate_sum + gate_w.astype(jnp.float32), up_sum + up_w.astype(jnp.float32),
                  down_sum + down_w.astype(jnp.float32))
        return wgrads, (out_total.astype(jnp.bfloat16), grad_total.astype(jnp.bfloat16))

    zeros = (jnp.zeros((EXPERTS, D, FF), jnp.float32), jnp.zeros((EXPERTS, D, FF), jnp.float32),
             jnp.zeros((EXPERTS, FF, D), jnp.float32))
    (gate_wgrad, up_wgrad, down_wgrad), (outs, grads) = lax.scan(
        one_group, zeros, jnp.arange(N_DP, dtype=jnp.int32))
    return (outs.reshape(TOKENS, D), grads.reshape(TOKENS, D), gate_wgrad, up_wgrad, down_wgrad)
```

```python
import jax
import jax.numpy as jnp
from jax import lax
from jax.experimental import pallas as pl
from jax.experimental.pallas import tpu as pltpu
from jax.sharding import PartitionSpec as P

MESH = pl.DeviceIdType.MESH
BF = jnp.bfloat16
F32 = jnp.float32
NZ, NY, NX = 8, 4, 4
T, C, D, F = 48, 16, 2048, 768
EXPERTS = NZ * NY
ROWS = NZ * NY * C
HD = D // 2
BACK = (7, 5, 6, 3, 4, 1, 2, 0)


def dot(a, b):
    return jnp.dot(a, b, preferred_element_type=F32)


def dot_cols(a, b):
    return lax.dot_general(a, b, (((1,), (1,)), ((), ())), preferred_element_type=F32)


def dot_rows(a, b):
    return lax.dot_general(a, b, (((0,), (0,)), ((), ())), preferred_element_type=F32)


def kernel(
    ids, probs, tok_hbm, cot_hbm, wg_hbm, wu_hbm, wd_hbm,
    layer_out, input_grad, gate_out, up_out, down_out,
    flat, ag, ai, sb, xg, eo, rback, relay, wg, wu, wd, gp, up, hid, gg, ug,
    zrecv, pg, pu, cr_a, cr_d, xh_a, xh_d, xf_a, xf_d,
    loc, ysend, yrecv, asend, arecv, isend, irecv, zsend, zrecv_sem, csend, crecv, xsend, xrecv,
):
    ex = lax.axis_index("expert")
    dp = lax.axis_index("dp")
    z, y = ex // NY, ex % NY
    x, core = dp // 2, dp % 2
    z_right = {"expert": (z + 1) % NZ * NY + y}
    z_left = {"expert": (z + NZ - 1) % NZ * NY + y}
    y_right = {"expert": z * NY + (y + 1) % NY}
    y_left = {"expert": z * NY + (y + NY - 1) % NY}
    x_right = {"dp": (x + 1) % NX * 2 + core}
    x_left = {"dp": (x + NX - 1) % NX * 2 + core}
    other = {"dp": x * 2 + 1 - core}

    started = []

    def send(src, dst, ssem, rsem, device):
        copy = pltpu.make_async_remote_copy(
            src_ref=src, dst_ref=dst, send_sem=ssem, recv_sem=rsem, device_id=device, device_id_type=MESH
        )
        copy.start()
        started.append(copy)
        return copy

    loads = {}
    for i, (src, dst) in enumerate(
        ((tok_hbm, ag.at[0, 0]), (cot_hbm, ag.at[1, 0]), (wg_hbm, wg), (wu_hbm, wu), (wd_hbm, wd))
    ):
        loads[i] = pltpu.make_async_copy(src, dst, loc.at[i])
        loads[i].start()

    barrier = pltpu.get_barrier_semaphore()
    for device in (z_right, z_left, y_right, y_left, x_right, x_left, other):
        pl.semaphore_signal(barrier, inc=1, device_id=device, device_id_type=MESH)

    flat[...] = jnp.full((128, 128), -1.0, F32)
    flat[0:T, 0:8] = ids[...].astype(F32)
    flat[0:T, 8:16] = probs[...]
    turned = flat[...].T
    expert_row = lax.broadcasted_iota(jnp.int32, (EXPERTS, 128), 0).astype(F32)
    named = jnp.zeros((EXPERTS, 128), F32)
    weight = jnp.zeros((EXPERTS, 128), F32)
    for k in range(8):
        same = turned[k : k + 1, :] == expert_row
        named = jnp.where(same, 1.0, named)
        weight = jnp.where(same, turned[8 + k : 9 + k, :], weight)
    before = (
        lax.broadcasted_iota(jnp.int32, (128, 128), 0) < lax.broadcasted_iota(jnp.int32, (128, 128), 1)
    ).astype(F32).astype(BF)
    place = jnp.where(named > 0.0, dot(named.astype(BF), before), -1.0)
    for p in range(NZ):
        ai[0, p, 0:4, :] = place[4 * p : 4 * p + 4, :]
        ai[0, p, 4:8, :] = weight[4 * p : 4 * p + 4, :]

    pl.semaphore_wait(barrier, 7)

    ag_copy = {}

    def ag_step(t, step):
        if step < 4:
            src_r, src_l = (0, 0) if step == 1 else (2 * step - 3, 2 * step - 2)
            r, l = 2 * step - 1, 2 * step
            ag_copy[t, r] = send(ag.at[t, src_r], ag.at[t, r], asend.at[t, r], arecv.at[t, r], z_right)
            ag_copy[t, l] = send(ag.at[t, src_l], ag.at[t, l], asend.at[t, l], arecv.at[t, l], z_left)
            if t == 0:
                ag_copy[2, r] = send(ai.at[src_r], ai.at[r], isend.at[r], irecv.at[r], z_right)
                ag_copy[2, l] = send(ai.at[src_l], ai.at[l], isend.at[l], irecv.at[l], z_left)
        else:
            ag_copy[t, 7] = send(
                ag.at[t, 5, :, pl.ds(0, HD)], ag.at[t, 7, :, pl.ds(0, HD)], asend.at[t, 7], arecv.at[t, 7], z_right
            )
            ag_copy[t, 0] = send(
                ag.at[t, 6, :, pl.ds(HD, HD)], ag.at[t, 7, :, pl.ds(HD, HD)], asend.at[t, 0], arecv.at[t, 0], z_left
            )
            if t == 0:
                ag_copy[2, 7] = send(ai.at[5], ai.at[7], isend.at[7], irecv.at[7], z_right)

    def ag_wait(t, slots):
        for s in slots:
            ag_copy[t, s].wait_recv()
            if s == 7:
                ag_copy[t, 0].wait_recv()
            if t == 0:
                ag_copy[2, s].wait_recv()

    def chooser(slot):
        table = ai[slot, z]
        line = lax.broadcasted_iota(jnp.int32, (8, 128), 0)
        want = lax.broadcasted_iota(jnp.int32, (C, 128), 0).astype(F32)
        picks, weights = [], []
        for r in range(NY):
            yy = (y + r) % NY
            place_row = jnp.sum(jnp.where(line == yy, table, 0.0), axis=0, keepdims=True)
            weight_row = jnp.sum(jnp.where(line == yy + 4, table, 0.0), axis=0, keepdims=True)
            hit = (place_row == want).astype(F32)
            picks.append(hit)
            weights.append(hit * weight_row)
        return jnp.concatenate(picks, axis=0), jnp.concatenate(weights, axis=0)

    y_copy = {}

    def rows(slot, r):
        return pl.ds(slot * 64 + r * C, C)

    def y_dst(t, slot, r):
        return xg.at[t, rows(slot, r)] if t < 2 else rback.at[t - 2, slot, r - 1]

    def y_src(t, slot, r):
        return sb.at[t, slot, r - 1] if t < 2 else eo.at[t - 2, rows(slot, r)]

    def y_send(t, slot):
        y_copy[t, slot, 0] = send(
            y_src(t, slot, 1), y_dst(t, slot, 3), ysend.at[t, slot, 0], yrecv.at[t, slot, 0], y_right
        )
        y_copy[t, slot, 1] = send(
            y_src(t, slot, 3), y_dst(t, slot, 1), ysend.at[t, slot, 1], yrecv.at[t, slot, 1], y_left
        )
        y_copy[t, slot, 2] = send(
            y_src(t, slot, 2), relay.at[t, slot], ysend.at[t, slot, 2], yrecv.at[t, slot, 2],
            y_right if slot % 2 == 0 else y_left,
        )

    def y_relay(t, *slots):
        for slot in slots:
            y_copy[t, slot, 2].wait_recv()
            y_copy[t, slot, 3] = send(
                relay.at[t, slot], y_dst(t, slot, 2), ysend.at[t, slot, 3], yrecv.at[t, slot, 3],
                y_right if slot % 2 == 0 else y_left,
            )

    def y_wait(t, *slots):
        for slot in slots:
            for i in (0, 1, 3):
                y_copy[t, slot, i].wait_recv()

    def select(t, *slots):
        for slot in slots:
            pick, weights = chooser(slot)
            chosen = dot(pick[:, :T].astype(BF), ag[t, slot])
            if t == 1:
                chosen = chosen * jnp.sum(weights, axis=1, keepdims=True)
            chosen = chosen.astype(BF)
            xg[t, rows(slot, 0), :] = chosen[0:C, :]
            for r in range(1, NY):
                sb[t, slot, r - 1] = chosen[r * C : (r + 1) * C, :]
            y_send(t, slot)

    def forward(c):
        band = pl.ds(c * 128, 128)

        @pl.loop(0, F // 256)
        def _(n):
            cols = pl.ds(pl.multiple_of(n * 256, 256), 256)
            g = dot(xg[0, band, :], wg[:, cols])
            u = dot(xg[0, band, :], wu[:, cols])
            gp[band, cols] = g
            up[band, cols] = u
            hid[band, cols] = (g * jax.nn.sigmoid(g) * u).astype(BF)

        @pl.loop(0, D // 256)
        def _(n):
            cols = pl.ds(pl.multiple_of(n * 256, 256), 256)
            eo[0, band, cols] = dot(hid[band, :], wd[:, cols]).astype(BF)

    def backward(c):
        band = pl.ds(c * 128, 128)

        @pl.loop(0, F // 256)
        def _(n):
            cols = pl.ds(pl.multiple_of(n * 256, 256), 256)
            hg = dot_cols(xg[1, band, :], wd[cols, :])
            g = gp[band, cols]
            s = jax.nn.sigmoid(g)
            gg[band, cols] = (hg * up[band, cols] * s * (1.0 + g * (1.0 - s))).astype(BF)
            ug[band, cols] = (hg * g * s).astype(BF)

    def row_grad(c):
        band = pl.ds(c * 128, 128)

        @pl.loop(0, D // 256)
        def _(n):
            cols = pl.ds(pl.multiple_of(n * 256, 256), 256)
            eo[1, band, cols] = (dot_cols(gg[band, :], wg[cols, :]) + dot_cols(ug[band, :], wu[cols, :])).astype(BF)

    z_copy = {}

    def combine(t, slot):
        pick, weights = chooser(slot)
        got = jnp.concatenate(
            [eo[t, rows(slot, 0), :], rback[t, slot, 0], rback[t, slot, 1], rback[t, slot, 2]], axis=0
        )
        if t == 1:
            return dot_rows(pick[:, :T].astype(BF), got)
        high = weights.astype(BF)
        low = (weights - high.astype(F32)).astype(BF)
        return dot_rows(high[:, :T], got) + dot_rows(low[:, :T], got)

    def z_step(t, slot):
        y_wait(t + 2, slot)
        total = combine(t, slot)
        if slot == 7:
            ag[t, 7] = total.astype(BF)
            z_copy[t, 0] = send(
                ag.at[t, 7, :, pl.ds(0, HD)], zrecv.at[t, 0, :, pl.ds(0, HD)],
                zsend.at[t, 0], zrecv_sem.at[t, 0], z_left,
            )
            z_copy[t, 4] = send(
                ag.at[t, 7, :, pl.ds(HD, HD)], zrecv.at[t, 0, :, pl.ds(HD, HD)],
                zsend.at[t, 4], zrecv_sem.at[t, 4], z_right,
            )
        elif slot > 0:
            leftward = slot % 2 == 1
            step = 3 - (slot - 1) // 2
            k = step if leftward else 4 + step
            z_copy[t, k - 1].wait_recv()
            if step == 1:
                half = pl.ds(0, HD) if leftward else pl.ds(HD, HD)
                lo = 0 if leftward else HD
                ag[t, slot] = total.astype(BF)
                ag[t, slot, :, half] = (total[:, lo : lo + HD] + zrecv[t, 0, :, half].astype(F32)).astype(BF)
            else:
                ag[t, slot] = (total + zrecv[t, k - 1].astype(F32)).astype(BF)
            z_copy[t, k] = send(
                ag.at[t, slot], zrecv.at[t, k], zsend.at[t, k], zrecv_sem.at[t, k], z_left if leftward else z_right
            )
        else:
            z_copy[t, 3].wait_recv()
            z_copy[t, 7].wait_recv()
            out = layer_out if t == 0 else input_grad
            out[...] = (total + zrecv[t, 3].astype(F32) + zrecv[t, 7].astype(F32)).astype(BF)

    parts = (wd, pg, pu)
    outs = (down_out, gate_out, up_out)
    deep = (F // 8, D // 8, D // 8)
    wide = (D, F, F)
    cr_of = (cr_d.at[0], cr_a.at[0], cr_a.at[1])
    xh_of = (xh_d.at[0], xh_a.at[0], xh_a.at[1])
    xf_of = (xf_d.at[0], xf_a.at[0], xf_a.at[1])
    core_copy, x_copy = {}, {}

    def band_of(w, k, c):
        return pl.multiple_of(((x + k) % NX * 2 + c) * deep[w], 32)

    def core_send(w, k):
        block = pl.ds(band_of(w, k, 1 - core), deep[w])
        core_copy[w, k] = send(
            parts[w].at[block], cr_of[w].at[k], csend.at[w, k], crecv.at[w, k], other
        )

    def wgrad_tile(w, k, c):
        grad = gg if w == 1 else ug
        start = pl.multiple_of(((x + k) % NX * 2 + c) * 256, 256)
        parts[w][pl.ds(start, 256), :] = dot_rows(xg[0, :, pl.ds(start, 256)], grad[...]).astype(BF)

    def wgrad(w, far):
        if w == 0:

            @pl.loop(0, D // 256)
            def _(n):
                cols = pl.ds(pl.multiple_of(n * 256, 256), 256)
                wd[:, cols] = dot_rows(hid[...], xg[1, :, cols]).astype(BF)

            for k in (2, 1, 3, 0):
                core_send(w, k)
        elif far:

            @pl.loop(0, NX)
            def _(k):
                wgrad_tile(w, k, 1 - core)

            for k in (2, 1, 3, 0):
                core_send(w, k)
        else:

            @pl.loop(0, NX)
            def _(k):
                wgrad_tile(w, k, core)

    def add_block(w, k, extra, finish=None):
        first = band_of(w, k, core)
        size = 32

        @pl.loop(0, deep[w] // size)
        def _(i):
            mine = pl.ds(pl.multiple_of(first + i * size, size), size)
            at = pl.ds(pl.multiple_of(i * size, size), size)
            total = parts[w][mine, :].astype(F32) + cr_of[w][k, at, :].astype(F32)
            for ref in extra:
                total = total + ref[at, :].astype(F32)
            if finish is None:
                parts[w][mine, :] = total.astype(BF)
            else:
                finish[at, :] = total

    def x_first(w):
        core_copy[w, 2].wait_recv()
        add_block(w, 2, ())
        half = wide[w] // 2
        block = pl.ds(band_of(w, 2, core), deep[w])
        x_copy[w, 0] = send(
            parts[w].at[block, pl.ds(0, half)], xh_of[w].at[0], xsend.at[w, 0], xrecv.at[w, 0], x_right
        )
        x_copy[w, 1] = send(
            parts[w].at[block, pl.ds(half, half)], xh_of[w].at[1], xsend.at[w, 1], xrecv.at[w, 1], x_left
        )

    def x_second(w):
        half = wide[w] // 2
        for i, k in ((0, 1), (1, 3)):
            core_copy[w, k].wait_recv()
            add_block(w, k, ())
            x_copy[w, i].wait_recv()
            first = band_of(w, k, core)

            @pl.loop(0, deep[w] // 32)
            def _(j):
                mine = pl.ds(pl.multiple_of(first + j * 32, 32), 32)
                at = pl.ds(pl.multiple_of(j * 32, 32), 32)
                cols = pl.ds(i * half, half)
                parts[w][mine, cols] = (
                    parts[w][mine, cols].astype(F32) + xh_of[w][i, at, :].astype(F32)
                ).astype(BF)

            x_copy[w, 2 + i] = send(
                parts[w].at[pl.ds(first, deep[w])], xf_of[w].at[i], xsend.at[w, 2 + i], xrecv.at[w, 2 + i],
                x_right if i == 0 else x_left,
            )

    def x_last(w):
        core_copy[w, 0].wait_recv()
        x_copy[w, 2].wait_recv()
        x_copy[w, 3].wait_recv()
        add_block(w, 0, (xf_of[w].at[0], xf_of[w].at[1]), outs[w])

    loads[0].wait()
    ag_step(0, 1)
    select(0, 0)
    loads[1].wait()
    select(1, 0)
    ag_wait(0, (1, 2))
    ag_step(0, 2)
    select(0, 1, 2)
    y_relay(0, 0)
    y_relay(1, 0)
    ag_wait(0, (3, 4))
    ag_step(0, 3)
    ag_step(1, 1)
    select(0, 3, 4)
    y_relay(0, 1, 2)
    ag_wait(0, (5, 6))
    ag_step(0, 4)
    select(0, 5, 6)
    ag_wait(1, (1, 2))
    ag_step(1, 2)
    y_relay(0, 3, 4)
    ag_wait(0, (7,))
    select(0, 7)
    select(1, 1, 2)
    y_relay(0, 5, 6)
    for i in (2, 3, 4):
        loads[i].wait()
    y_wait(0, 0, 1)
    forward(0)
    ag_wait(1, (3, 4))
    ag_step(1, 3)
    select(1, 3, 4)
    y_relay(0, 7)
    y_relay(1, 1, 2)
    y_wait(0, 2, 3)
    forward(1)
    ag_wait(1, (5, 6))
    ag_step(1, 4)
    select(1, 5, 6)
    y_relay(1, 3, 4)
    y_wait(0, 4, 5)
    forward(2)
    ag_wait(1, (7,))
    select(1, 7)
    y_relay(1, 5, 6)
    y_wait(0, 6, 7)
    forward(3)
    y_relay(1, 7)
    for key, copy in ag_copy.items():
        copy.wait_send()
    for s in (7, 5, 6):
        y_send(2, s)
    y_wait(1, 0, 1)
    backward(0)
    y_wait(1, 2, 3)
    backward(1)
    y_wait(1, 4, 5)
    backward(2)
    y_wait(1, 6, 7)
    backward(3)
    y_relay(2, 7)
    y_send(2, 3)
    y_send(2, 4)
    y_relay(2, 5, 6)
    wgrad(0, True)
    y_relay(2, 3)
    y_send(2, 1)
    y_send(2, 2)
    y_send(2, 0)
    y_relay(2, 4)
    z_step(0, 7)
    wgrad(1, True)
    x_first(0)
    wgrad(1, False)
    y_relay(2, 1, 2)
    z_step(0, 5)
    z_step(0, 6)
    wgrad(2, True)
    x_second(0)
    x_first(1)
    y_relay(2, 0)
    z_step(0, 3)
    z_step(0, 4)
    row_grad(3)
    row_grad(2)
    for s in (7, 5, 6):
        y_send(3, s)
    wgrad(2, False)
    z_step(0, 1)
    z_step(0, 2)
    row_grad(1)
    y_relay(3, 7)
    y_send(3, 3)
    y_send(3, 4)
    row_grad(0)
    x_second(1)
    x_first(2)
    z_step(0, 0)
    y_relay(3, 5, 6)
    for s in (1, 2, 0):
        y_send(3, s)
    x_last(0)
    z_step(1, 7)
    y_relay(3, 3, 4)
    z_step(1, 5)
    z_step(1, 6)
    x_second(2)
    y_relay(3, 1, 2)
    z_step(1, 3)
    z_step(1, 4)
    x_last(1)
    y_relay(3, 0)
    z_step(1, 1)
    z_step(1, 2)
    x_last(2)
    z_step(1, 0)

    early = [id(copy) for copy in ag_copy.values()]
    for copy in started:
        if id(copy) not in early:
            copy.wait_send()


def shards(tokens, expert_ids, gate_probs, out_cot, w_gate, w_up, w_down):
    vmem = pl.BlockSpec(memory_space=pltpu.VMEM)
    hbm = pl.BlockSpec(memory_space=pl.ANY)
    dma = pltpu.SemaphoreType.DMA
    V = pltpu.VMEM
    shape = jax.ShapeDtypeStruct
    layer_out, input_grad, gate, up, down = pl.pallas_call(
        kernel,
        out_shape=(
            shape((T, D), BF),
            shape((T, D), BF),
            shape((D // 8, F), F32),
            shape((D // 8, F), F32),
            shape((F // 8, D), F32),
        ),
        in_specs=[vmem, vmem, hbm, hbm, hbm, hbm, hbm],
        out_specs=(vmem,) * 5,
        scratch_shapes=[
            V((128, 128), F32),
            V((2, NZ, T, D), BF),
            V((NZ, NZ, 8, 128), F32),
            V((2, NZ, 3, C, D), BF),
            V((2, ROWS, D), BF),
            V((2, ROWS, D), BF),
            V((2, NZ, 3, C, D), BF),
            V((4, NZ, C, D), BF),
            V((D, F), BF),
            V((D, F), BF),
            V((F, D), BF),
            V((ROWS, F), F32),
            V((ROWS, F), F32),
            V((ROWS, F), BF),
            V((ROWS, F), BF),
            V((ROWS, F), BF),
            V((2, NZ, T, D), BF),
            V((D, F), BF),
            V((D, F), BF),
            V((2, NX, D // 8, F), BF),
            V((1, NX, F // 8, D), BF),
            V((2, 2, D // 8, F // 2), BF),
            V((1, 2, F // 8, D // 2), BF),
            V((2, 2, D // 8, F), BF),
            V((1, 2, F // 8, D), BF),
            dma((5,)),
            dma((4, NZ, 4)),
            dma((4, NZ, 4)),
            dma((2, NZ)),
            dma((2, NZ)),
            dma((NZ,)),
            dma((NZ,)),
            dma((2, 8)),
            dma((2, 8)),
            dma((3, NX)),
            dma((3, NX)),
            dma((3, 4)),
            dma((3, 4)),
        ],
        compiler_params=pltpu.CompilerParams(
            collective_id=0, has_side_effects=True, vmem_limit_bytes=66_900_000
        ),
        name="expert_layer",
    )(expert_ids, gate_probs, tokens, out_cot, w_gate[0], w_up[0], w_down[0])
    return (layer_out, input_grad, gate[None], up[None], down[None])


def solution(mesh):
    placed = (
        P(("dp", "expert"), None),
        P(("dp", "expert"), None),
        P(("dp", "expert"), None),
        P(("dp", "expert"), None),
        P("expert", None, None),
        P("expert", None, None),
        P("expert", None, None),
    )
    return jax.shard_map(
        shards,
        mesh=mesh,
        in_specs=placed,
        out_specs=(
            P(("dp", "expert"), None),
            P(("dp", "expert"), None),
            P("expert", "dp", None),
            P("expert", "dp", None),
            P("expert", "dp", None),
        ),
        check_vma=False,
    )
```

```python
import jax
import jax.numpy as jnp
from jax import lax
from jax.experimental import pallas as pl
from jax.experimental.pallas import tpu as pltpu
from jax.sharding import PartitionSpec as P

MESH = pl.DeviceIdType.MESH
BF = jnp.bfloat16
F32 = jnp.float32
NZ, NY, NX = 8, 4, 4
T, C, D, F = 48, 16, 2048, 768
EXPERTS = NZ * NY
ROWS = NZ * NY * C
HD = D // 2
BACK = (7, 5, 6, 3, 4, 1, 2, 0)


def dot(a, b):
    return jnp.dot(a, b, preferred_element_type=F32)


def dot_cols(a, b):
    return lax.dot_general(a, b, (((1,), (1,)), ((), ())), preferred_element_type=F32)


def dot_rows(a, b):
    return lax.dot_general(a, b, (((0,), (0,)), ((), ())), preferred_element_type=F32)


def kernel(
    ids_hbm, probs_hbm, tok_hbm, cot_hbm, wg_hbm, wu_hbm, wd_hbm,
    layer_out, input_grad, gate_out, up_out, down_out,
    ids, probs, ag, ai, sb, xg, eo, rback, relay, wg, wu, wd, gp, up, hid, gg, ug,
    zrecv, pg, pu, cr_a, cr_d, xh_a, xh_d, xf_a, xf_d,
    loc, ysend, yrecv, asend, arecv, isend, irecv, zsend, zrecv_sem, csend, crecv, xsend, xrecv,
):
    ex = lax.axis_index("expert")
    dp = lax.axis_index("dp")
    z, y = ex // NY, ex % NY
    x, core = dp // 2, dp % 2
    z_right = {"expert": (z + 1) % NZ * NY + y}
    z_left = {"expert": (z + NZ - 1) % NZ * NY + y}
    y_right = {"expert": z * NY + (y + 1) % NY}
    y_left = {"expert": z * NY + (y + NY - 1) % NY}
    x_right = {"dp": (x + 1) % NX * 2 + core}
    x_left = {"dp": (x + NX - 1) % NX * 2 + core}
    other = {"dp": x * 2 + 1 - core}

    started = []

    def send(src, dst, ssem, rsem, device):
        copy = pltpu.make_async_remote_copy(
            src_ref=src, dst_ref=dst, send_sem=ssem, recv_sem=rsem, device_id=device, device_id_type=MESH
        )
        copy.start()
        started.append(copy)
        return copy

    loads = {}
    for i, (src, dst) in enumerate(
        (
            (ids_hbm, ids), (probs_hbm, probs), (tok_hbm, ag.at[0, 0]), (cot_hbm, ag.at[1, 0]),
            (wg_hbm, wg), (wu_hbm, wu), (wd_hbm, wd),
        )
    ):
        loads[i] = pltpu.make_async_copy(src, dst, loc.at[i])
        loads[i].start()

    barrier = pltpu.get_barrier_semaphore()
    for device in (z_right, z_left, y_right, y_left, x_right, x_left, other):
        pl.semaphore_signal(barrier, inc=1, device_id=device, device_id_type=MESH)

    loads[0].wait()
    loads[1].wait()
    fill = jnp.full((8, 128 - T), -1, jnp.int32)
    chosen_ids = jnp.concatenate([ids[...], fill], axis=1)
    chosen_probs = jnp.concatenate([probs[...], fill.astype(F32)], axis=1)
    expert_row = lax.broadcasted_iota(jnp.int32, (EXPERTS, 128), 0)
    named = jnp.zeros((EXPERTS, 128), F32)
    weight = jnp.zeros((EXPERTS, 128), F32)
    for k in range(8):
        same = chosen_ids[k : k + 1, :] == expert_row
        named = jnp.where(same, 1.0, named)
        weight = jnp.where(same, chosen_probs[k : k + 1, :], weight)
    before = (
        lax.broadcasted_iota(jnp.int32, (128, 128), 0) < lax.broadcasted_iota(jnp.int32, (128, 128), 1)
    ).astype(F32).astype(BF)
    place = jnp.where(named > 0.0, dot(named.astype(BF), before), -1.0)
    for p in range(NZ):
        ai[0, p, 0:4, :] = place[4 * p : 4 * p + 4, :]
        ai[0, p, 4:8, :] = weight[4 * p : 4 * p + 4, :]

    pl.semaphore_wait(barrier, 7)

    loaded = set()

    ag_copy = {}

    def ag_step(t, step):
        if step < 4:
            src_r, src_l = (0, 0) if step == 1 else (2 * step - 3, 2 * step - 2)
            r, l = 2 * step - 1, 2 * step
            ag_copy[t, r] = send(ag.at[t, src_r], ag.at[t, r], asend.at[t, r], arecv.at[t, r], z_right)
            ag_copy[t, l] = send(ag.at[t, src_l], ag.at[t, l], asend.at[t, l], arecv.at[t, l], z_left)
            if t == 0:
                ag_copy[2, r] = send(ai.at[src_r], ai.at[r], isend.at[r], irecv.at[r], z_right)
                ag_copy[2, l] = send(ai.at[src_l], ai.at[l], isend.at[l], irecv.at[l], z_left)
        else:
            ag_copy[t, 7] = send(
                ag.at[t, 5, :, pl.ds(0, HD)], ag.at[t, 7, :, pl.ds(0, HD)], asend.at[t, 7], arecv.at[t, 7], z_right
            )
            ag_copy[t, 0] = send(
                ag.at[t, 6, :, pl.ds(HD, HD)], ag.at[t, 7, :, pl.ds(HD, HD)], asend.at[t, 0], arecv.at[t, 0], z_left
            )
            if t == 0:
                ag_copy[2, 7] = send(ai.at[5], ai.at[7], isend.at[7], irecv.at[7], z_right)

    seen = set()

    def once(t, s):
        if (t, s) not in seen:
            seen.add((t, s))
            ag_copy[t, s].wait_recv()

    def ag_wait(t, slots):
        for s in slots:
            once(t, s)
            if s == 7:
                once(t, 0)
            once(2, s)

    def gather(t, step):
        if step == 1:
            if t not in loaded:
                loads[2 + t].wait()
                loaded.add(t)
        else:
            ag_wait(t, (2 * step - 3, 2 * step - 2))
        ag_step(t, step)

    def chooser(slot):
        table = ai[slot, z]
        line = lax.broadcasted_iota(jnp.int32, (8, 128), 0)
        want = lax.broadcasted_iota(jnp.int32, (C, 128), 0).astype(F32)
        picks, weights = [], []
        for r in range(NY):
            yy = (y + r) % NY
            place_row = jnp.sum(jnp.where(line == yy, table, 0.0), axis=0, keepdims=True)
            weight_row = jnp.sum(jnp.where(line == yy + 4, table, 0.0), axis=0, keepdims=True)
            hit = (place_row == want).astype(F32)
            picks.append(hit)
            weights.append(hit * weight_row)
        return jnp.concatenate(picks, axis=0), jnp.concatenate(weights, axis=0)

    y_copy = {}

    def rows(slot, r):
        return pl.ds(slot * 64 + r * C, C)

    def y_dst(t, slot, r):
        return xg.at[t, rows(slot, r)] if t < 2 else rback.at[t - 2, slot, r - 1]

    def y_src(t, slot, r):
        return sb.at[t, slot, r - 1] if t < 2 else eo.at[t - 2, rows(slot, r)]

    def y_send(t, slot):
        y_copy[t, slot, 0] = send(
            y_src(t, slot, 1), y_dst(t, slot, 3), ysend.at[t, slot, 0], yrecv.at[t, slot, 0], y_right
        )
        y_copy[t, slot, 1] = send(
            y_src(t, slot, 3), y_dst(t, slot, 1), ysend.at[t, slot, 1], yrecv.at[t, slot, 1], y_left
        )
        y_copy[t, slot, 2] = send(
            y_src(t, slot, 2), relay.at[t, slot], ysend.at[t, slot, 2], yrecv.at[t, slot, 2],
            y_right if slot % 2 == 0 else y_left,
        )

    def y_relay(t, *slots):
        for slot in slots:
            y_copy[t, slot, 2].wait_recv()
            y_copy[t, slot, 3] = send(
                relay.at[t, slot], y_dst(t, slot, 2), ysend.at[t, slot, 3], yrecv.at[t, slot, 3],
                y_right if slot % 2 == 0 else y_left,
            )

    def y_wait(t, *slots):
        for slot in slots:
            for i in (0, 1, 3):
                y_copy[t, slot, i].wait_recv()

    def choose(t, slot):
        if slot > 0:
            ag_wait(t, (slot,))
        elif t not in loaded:
            loads[2 + t].wait()
            loaded.add(t)
        pick, weights = chooser(slot)
        chosen = dot(pick[:, :T].astype(BF), ag[t, slot])
        if t == 1:
            chosen = chosen * jnp.sum(weights, axis=1, keepdims=True)
        chosen = chosen.astype(BF)
        xg[t, rows(slot, 0), :] = chosen[0:C, :]
        for r in range(1, NY):
            sb[t, slot, r - 1] = chosen[r * C : (r + 1) * C, :]
        y_send(t, slot)

    down_ready = []

    def forward(c):
        y_wait(0, 2 * c, 2 * c + 1)
        if c == 0:
            loads[4].wait()
            loads[5].wait()
        band = pl.ds(c * 128, 128)

        @pl.loop(0, F // 256)
        def _(n):
            cols = pl.ds(pl.multiple_of(n * 256, 256), 256)
            g = dot(xg[0, band, :], wg[:, cols])
            u = dot(xg[0, band, :], wu[:, cols])
            gp[band, cols] = g
            up[band, cols] = u
            hid[band, cols] = (g * jax.nn.sigmoid(g) * u).astype(BF)

    def down(c):
        if not down_ready:
            loads[6].wait()
            down_ready.append(c)
        band = pl.ds(c * 128, 128)

        @pl.loop(0, D // 256)
        def _(n):
            cols = pl.ds(pl.multiple_of(n * 256, 256), 256)
            eo[0, band, cols] = dot(hid[band, :], wd[:, cols]).astype(BF)

    def backward(c):
        y_wait(1, 2 * c, 2 * c + 1)
        if not down_ready:
            loads[6].wait()
            down_ready.append(c)
        band = pl.ds(c * 128, 128)

        @pl.loop(0, F // 256)
        def _(n):
            cols = pl.ds(pl.multiple_of(n * 256, 256), 256)
            hg = dot_cols(xg[1, band, :], wd[cols, :])
            g = gp[band, cols]
            s = jax.nn.sigmoid(g)
            gg[band, cols] = (hg * up[band, cols] * s * (1.0 + g * (1.0 - s))).astype(BF)
            ug[band, cols] = (hg * g * s).astype(BF)

    def row_grad(c):
        band = pl.ds(c * 128, 128)

        @pl.loop(0, D // 256)
        def _(n):
            cols = pl.ds(pl.multiple_of(n * 256, 256), 256)
            eo[1, band, cols] = (dot_cols(gg[band, :], wg[cols, :]) + dot_cols(ug[band, :], wu[cols, :])).astype(BF)

    z_copy = {}

    def combine(t, slot):
        pick, weights = chooser(slot)
        got = jnp.concatenate(
            [eo[t, rows(slot, 0), :], rback[t, slot, 0], rback[t, slot, 1], rback[t, slot, 2]], axis=0
        )
        if t == 1:
            return dot_rows(pick[:, :T].astype(BF), got)
        high = weights.astype(BF)
        low = (weights - high.astype(F32)).astype(BF)
        return dot_rows(high[:, :T], got) + dot_rows(low[:, :T], got)

    def z_step(t, slot):
        y_wait(t + 2, slot)
        total = combine(t, slot)
        if slot == 7:
            for key, copy in ag_copy.items():
                if key[0] == t:
                    copy.wait_send()
            ag[t, 7] = total.astype(BF)
            z_copy[t, 0] = send(
                ag.at[t, 7, :, pl.ds(0, HD)], zrecv.at[t, 0, :, pl.ds(0, HD)],
                zsend.at[t, 0], zrecv_sem.at[t, 0], z_left,
            )
            z_copy[t, 4] = send(
                ag.at[t, 7, :, pl.ds(HD, HD)], zrecv.at[t, 0, :, pl.ds(HD, HD)],
                zsend.at[t, 4], zrecv_sem.at[t, 4], z_right,
            )
        elif slot > 0:
            leftward = slot % 2 == 1
            step = 3 - (slot - 1) // 2
            k = step if leftward else 4 + step
            z_copy[t, k - 1].wait_recv()
            if step == 1:
                half = pl.ds(0, HD) if leftward else pl.ds(HD, HD)
                lo = 0 if leftward else HD
                ag[t, slot] = total.astype(BF)
                ag[t, slot, :, half] = (total[:, lo : lo + HD] + zrecv[t, 0, :, half].astype(F32)).astype(BF)
            else:
                ag[t, slot] = (total + zrecv[t, k - 1].astype(F32)).astype(BF)
            z_copy[t, k] = send(
                ag.at[t, slot], zrecv.at[t, k], zsend.at[t, k], zrecv_sem.at[t, k], z_left if leftward else z_right
            )
        else:
            z_copy[t, 3].wait_recv()
            z_copy[t, 7].wait_recv()
            out = layer_out if t == 0 else input_grad
            out[...] = (total + zrecv[t, 3].astype(F32) + zrecv[t, 7].astype(F32)).astype(BF)

    parts = (wd, pg, pu)
    outs = (down_out, gate_out, up_out)
    deep = (F // 8, D // 8, D // 8)
    wide = (D, F, F)
    cr_of = (cr_d.at[0], cr_a.at[0], cr_a.at[1])
    xh_of = (xh_d.at[0], xh_a.at[0], xh_a.at[1])
    xf_of = (xf_d.at[0], xf_a.at[0], xf_a.at[1])
    core_copy, x_copy = {}, {}

    def band_of(w, k, c):
        return pl.multiple_of(((x + k) % NX * 2 + c) * deep[w], 32)

    def core_send(w, k):
        block = pl.ds(band_of(w, k, 1 - core), deep[w])
        core_copy[w, k] = send(
            parts[w].at[block], cr_of[w].at[k], csend.at[w, k], crecv.at[w, k], other
        )

    def wgrad_tile(w, k, c):
        grad = gg if w == 1 else ug
        start = pl.multiple_of(((x + k) % NX * 2 + c) * 256, 256)
        parts[w][pl.ds(start, 256), :] = dot_rows(xg[0, :, pl.ds(start, 256)], grad[...]).astype(BF)

    def wgrad(w, far):
        if w == 0:

            @pl.loop(0, D // 256)
            def _(n):
                cols = pl.ds(pl.multiple_of(n * 256, 256), 256)
                wd[:, cols] = dot_rows(hid[...], xg[1, :, cols]).astype(BF)

            for k in (2, 1, 3, 0):
                core_send(w, k)
        elif far:

            @pl.loop(0, NX)
            def _(k):
                wgrad_tile(w, k, 1 - core)

            for k in (2, 1, 3, 0):
                core_send(w, k)
        else:

            @pl.loop(0, NX)
            def _(k):
                wgrad_tile(w, k, core)

    def add_block(w, k, extra, finish=None):
        first = band_of(w, k, core)
        size = 32

        @pl.loop(0, deep[w] // size)
        def _(i):
            mine = pl.ds(pl.multiple_of(first + i * size, size), size)
            at = pl.ds(pl.multiple_of(i * size, size), size)
            total = parts[w][mine, :].astype(F32) + cr_of[w][k, at, :].astype(F32)
            for ref in extra:
                total = total + ref[at, :].astype(F32)
            if finish is None:
                parts[w][mine, :] = total.astype(BF)
            else:
                finish[at, :] = total

    def x_first(w):
        core_copy[w, 2].wait_recv()
        add_block(w, 2, ())
        half = wide[w] // 2
        block = pl.ds(band_of(w, 2, core), deep[w])
        x_copy[w, 0] = send(
            parts[w].at[block, pl.ds(0, half)], xh_of[w].at[0], xsend.at[w, 0], xrecv.at[w, 0], x_right
        )
        x_copy[w, 1] = send(
            parts[w].at[block, pl.ds(half, half)], xh_of[w].at[1], xsend.at[w, 1], xrecv.at[w, 1], x_left
        )

    def x_second(w, i):
        half = wide[w] // 2
        k = (1, 3)[i]
        core_copy[w, k].wait_recv()
        add_block(w, k, ())
        x_copy[w, i].wait_recv()
        first = band_of(w, k, core)

        @pl.loop(0, deep[w] // 32)
        def _(j):
            mine = pl.ds(pl.multiple_of(first + j * 32, 32), 32)
            at = pl.ds(pl.multiple_of(j * 32, 32), 32)
            cols = pl.ds(i * half, half)
            parts[w][mine, cols] = (
                parts[w][mine, cols].astype(F32) + xh_of[w][i, at, :].astype(F32)
            ).astype(BF)

        x_copy[w, 2 + i] = send(
            parts[w].at[pl.ds(first, deep[w])], xf_of[w].at[i], xsend.at[w, 2 + i], xrecv.at[w, 2 + i],
            x_right if i == 0 else x_left,
        )

    def x_last(w):
        core_copy[w, 0].wait_recv()
        x_copy[w, 2].wait_recv()
        x_copy[w, 3].wait_recv()
        add_block(w, 0, (xf_of[w].at[0], xf_of[w].at[1]), outs[w])

    for step in (
        (gather, 0, 1), (choose, 1, 0), (gather, 1, 1), (choose, 0, 0), (choose, 0, 2), (gather, 0, 2),
        (choose, 0, 1), (choose, 1, 1), (gather, 1, 2), (y_relay, 0, 0), (y_relay, 0, 1), (choose, 1, 2),
        (choose, 0, 3), (y_relay, 1, 0), (gather, 0, 3), (forward, 0), (y_relay, 0, 2), (y_relay, 1, 1),
        (choose, 0, 4), (choose, 1, 3), (choose, 1, 4), (gather, 0, 4), (gather, 1, 3), (y_relay, 0, 3),
        (backward, 0), (choose, 0, 5), (row_grad, 0), (choose, 0, 6), (y_relay, 1, 2), (y_relay, 0, 4),
        (y_relay, 1, 4), (y_relay, 1, 3), (forward, 1), (down, 0), (y_relay, 0, 5), (choose, 0, 7), (gather, 1, 4),
        (y_relay, 0, 6), (choose, 1, 5), (backward, 1), (row_grad, 1), (y_relay, 0, 7), (choose, 1, 7), (down, 1),
        (choose, 1, 6), (y_relay, 1, 5), (forward, 2), (forward, 3), (y_relay, 1, 7), (down, 2), (y_relay, 1, 6),
        (y_send, 2, 4), (down, 3), (y_send, 2, 7), (backward, 2), (y_send, 2, 6), (backward, 3), (y_send, 2, 5),
        (wgrad, 1, 1), (row_grad, 3), (y_send, 3, 7), (wgrad, 1, 0), (y_send, 3, 6), (y_send, 2, 3), (y_relay, 2, 7),
        (x_first, 1), (y_relay, 2, 6), (wgrad, 2, 1), (row_grad, 2), (y_relay, 3, 7), (wgrad, 2, 0),
        (x_second, 1, 0), (y_send, 3, 5), (y_relay, 2, 5), (x_second, 1, 1), (y_send, 3, 4), (wgrad, 0, 1),
        (y_send, 2, 2), (y_relay, 3, 6), (z_step, 0, 7), (y_relay, 3, 5), (y_send, 3, 3), (y_relay, 2, 3),
        (z_step, 1, 7), (x_first, 0), (z_step, 0, 6), (z_step, 0, 5), (y_send, 2, 1), (x_first, 2), (x_last, 1),
        (y_relay, 2, 4), (y_relay, 3, 4), (z_step, 1, 6), (z_step, 1, 5), (y_relay, 2, 2), (x_second, 0, 0),
        (x_second, 0, 1), (y_relay, 3, 3), (y_send, 2, 0), (z_step, 0, 3), (y_send, 3, 1), (z_step, 0, 4),
        (y_relay, 2, 1), (y_send, 3, 2), (x_second, 2, 1), (z_step, 1, 4), (z_step, 1, 3), (y_relay, 2, 0),
        (z_step, 0, 2), (y_relay, 3, 1), (y_send, 3, 0), (y_relay, 3, 2), (x_second, 2, 0), (z_step, 0, 1),
        (z_step, 1, 1), (y_relay, 3, 0), (x_last, 0), (z_step, 1, 2), (z_step, 0, 0), (x_last, 2), (z_step, 1, 0),
    ):
        step[0](*step[1:])

    early = [id(copy) for key, copy in ag_copy.items() if key[0] < 2]
    for copy in started:
        if id(copy) not in early:
            copy.wait_send()


def store(*refs):
    copies = [pltpu.make_async_copy(refs[i], refs[5 + i], refs[10].at[i]) for i in range(5)]
    for copy in copies:
        copy.start()
    for copy in copies:
        copy.wait()


def shards(tokens, expert_ids, gate_probs, out_cot, w_gate, w_up, w_down):
    vmem = pl.BlockSpec(memory_space=pltpu.VMEM)
    hbm = pl.BlockSpec(memory_space=pl.ANY)
    dma = pltpu.SemaphoreType.DMA
    V = pltpu.VMEM
    results = pl.pallas_call(
        kernel,
        out_shape=(
            V((T, D), BF),
            V((T, D), BF),
            V((D // 8, F), F32),
            V((D // 8, F), F32),
            V((F // 8, D), F32),
        ),
        in_specs=[hbm] * 7,
        out_specs=(vmem,) * 5,
        scratch_shapes=[
            V((8, T), jnp.int32),
            V((8, T), F32),
            V((2, NZ, T, D), BF),
            V((NZ, NZ, 8, 128), F32),
            V((2, NZ, 3, C, D), BF),
            V((2, ROWS, D), BF),
            V((2, ROWS, D), BF),
            V((2, NZ, 3, C, D), BF),
            V((4, NZ, C, D), BF),
            V((D, F), BF),
            V((D, F), BF),
            V((F, D), BF),
            V((ROWS, F), F32),
            V((ROWS, F), F32),
            V((ROWS, F), BF),
            V((ROWS, F), BF),
            V((ROWS, F), BF),
            V((2, NZ, T, D), BF),
            V((D, F), BF),
            V((D, F), BF),
            V((2, NX, D // 8, F), BF),
            V((1, NX, F // 8, D), BF),
            V((2, 2, D // 8, F // 2), BF),
            V((1, 2, F // 8, D // 2), BF),
            V((2, 2, D // 8, F), BF),
            V((1, 2, F // 8, D), BF),
            dma((7,)),
            dma((4, NZ, 4)),
            dma((4, NZ, 4)),
            dma((2, NZ)),
            dma((2, NZ)),
            dma((NZ,)),
            dma((NZ,)),
            dma((2, 8)),
            dma((2, 8)),
            dma((3, NX)),
            dma((3, NX)),
            dma((3, 4)),
            dma((3, 4)),
        ],
        compiler_params=pltpu.CompilerParams(
            collective_id=0, has_side_effects=True, vmem_limit_bytes=63_900_000
        ),
        name="expert_layer",
    )(expert_ids.T, gate_probs.T, tokens, out_cot, w_gate[0], w_up[0], w_down[0])
    layer_out, input_grad, gate, up, down = pl.pallas_call(
        store,
        out_shape=tuple(jax.ShapeDtypeStruct(r.shape, r.dtype) for r in results),
        in_specs=[hbm] * 5,
        out_specs=(hbm,) * 5,
        scratch_shapes=[dma((5,))],
        compiler_params=pltpu.CompilerParams(vmem_limit_bytes=1 << 20),
        name="store",
    )(*results)
    return (layer_out, input_grad, gate[None], up[None], down[None])


def solution(mesh):
    placed = (
        P(("dp", "expert"), None),
        P(("dp", "expert"), None),
        P(("dp", "expert"), None),
        P(("dp", "expert"), None),
        P("expert", None, None),
        P("expert", None, None),
        P("expert", None, None),
    )
    return jax.shard_map(
        shards,
        mesh=mesh,
        in_specs=placed,
        out_specs=(
            P(("dp", "expert"), None),
            P(("dp", "expert"), None),
            P("expert", "dp", None),
            P("expert", "dp", None),
            P("expert", "dp", None),
        ),
        check_vma=False,
    )
```

```python
import jax
import jax.numpy as jnp
from jax import lax
from jax.experimental import pallas as pl
from jax.experimental.pallas import tpu as pltpu
from jax.sharding import PartitionSpec as P

MESH = pl.DeviceIdType.MESH
BF = jnp.bfloat16
F32 = jnp.float32
NZ, NY, NX = 8, 4, 4
T, C, D, F = 48, 16, 2048, 768
EXPERTS = NZ * NY
ROWS = NZ * NY * C
HD = D // 2
BACK = (7, 5, 6, 3, 4, 1, 2, 0)


def dot(a, b):
    return jnp.dot(a, b, preferred_element_type=F32)


def dot_cols(a, b):
    return lax.dot_general(a, b, (((1,), (1,)), ((), ())), preferred_element_type=F32)


def dot_rows(a, b):
    return lax.dot_general(a, b, (((0,), (0,)), ((), ())), preferred_element_type=F32)


def kernel(
    ids_hbm, probs_hbm, tok_hbm, cot_hbm, wg_hbm, wu_hbm, wd_hbm,
    layer_out, input_grad, gate_out, up_out, down_out,
    ids, probs, chooser_rows, far_send, far_relay, far_info, drelay, dland, ag, ai, sb, xg, eo, rback, relay, wg, wu, wd, gp, up, hid, gg, ug,
    zrecv, pg, pu, cr_a, cr_d, xh_a, xh_d, xf_a, xf_d,
    loc, ysend, yrecv, asend, arecv, isend, irecv, zsend, zrecv_sem, csend, crecv, xsend, xrecv, fsend, frecv,
    dsend, drecv,
):
    ex = lax.axis_index("expert")
    dp = lax.axis_index("dp")
    z, y = ex // NY, ex % NY
    x, core = dp // 2, dp % 2
    z_right = {"expert": (z + 1) % NZ * NY + y}
    z_left = {"expert": (z + NZ - 1) % NZ * NY + y}
    z_right2 = {"expert": (z + 2) % NZ * NY + y}
    z_left2 = {"expert": (z + NZ - 2) % NZ * NY + y}
    y_right = {"expert": z * NY + (y + 1) % NY}
    y_left = {"expert": z * NY + (y + NY - 1) % NY}
    x_right = {"dp": (x + 1) % NX * 2 + core}
    x_left = {"dp": (x + NX - 1) % NX * 2 + core}
    other = {"dp": x * 2 + 1 - core}

    def line_of(table, index):
        line = lax.broadcasted_iota(jnp.int32, (8, 128), 0)
        return jnp.sum(jnp.where(line == index, table, 0.0), axis=0, keepdims=True)

    started = []

    def send(src, dst, ssem, rsem, device):
        copy = pltpu.make_async_remote_copy(
            src_ref=src, dst_ref=dst, send_sem=ssem, recv_sem=rsem, device_id=device, device_id_type=MESH
        )
        copy.start()
        started.append(copy)
        return copy

    loads = {}
    for i, (src, dst) in enumerate(
        (
            (ids_hbm, ids), (probs_hbm, probs), (tok_hbm, ag.at[0, 0]), (cot_hbm, ag.at[1, 0]),
            (wg_hbm, wg), (wu_hbm, wu), (wd_hbm, wd),
        )
    ):
        loads[i] = pltpu.make_async_copy(src, dst, loc.at[i])
        loads[i].start()

    barrier = pltpu.get_barrier_semaphore()
    for device in (z_right, z_left, z_right2, z_left2, y_right, y_left, x_right, x_left, other):
        pl.semaphore_signal(barrier, inc=1, device_id=device, device_id_type=MESH)

    loads[0].wait()
    loads[1].wait()
    fill = jnp.full((8, 128 - T), -1, jnp.int32)
    chosen_ids = jnp.concatenate([ids[...], fill], axis=1)
    chosen_probs = jnp.concatenate([probs[...], fill.astype(F32)], axis=1)
    expert_row = lax.broadcasted_iota(jnp.int32, (EXPERTS, 128), 0)
    named = jnp.zeros((EXPERTS, 128), F32)
    weight = jnp.zeros((EXPERTS, 128), F32)
    for k in range(8):
        same = chosen_ids[k : k + 1, :] == expert_row
        named = jnp.where(same, 1.0, named)
        weight = jnp.where(same, chosen_probs[k : k + 1, :], weight)
    before = (
        lax.broadcasted_iota(jnp.int32, (128, 128), 0) < lax.broadcasted_iota(jnp.int32, (128, 128), 1)
    ).astype(F32).astype(BF)
    place = jnp.where(named > 0.0, dot(named.astype(BF), before), -1.0)
    for p in range(NZ):
        ai[0, p, 0:4, :] = place[4 * p : 4 * p + 4, :]
        ai[0, p, 4:8, :] = weight[4 * p : 4 * p + 4, :]

    for i, shift in enumerate((0, 1, NZ - 1, 2, NZ - 2)):
        table = ai[0, (z + shift) % NZ]
        far_send[2 * i : 2 * i + 1, :] = line_of(table, (y + 2) % NY)
        far_send[2 * i + 1 : 2 * i + 2, :] = line_of(table, (y + 2) % NY + 4)
    far_send[10:16, :] = jnp.zeros((6, 128), F32)

    pl.semaphore_wait(barrier, 9)

    loaded = set()

    ag_copy = {}

    def ag_step(t, step):
        if step < 4:
            src_r, src_l = (0, 0) if step == 1 else (2 * step - 3, 2 * step - 2)
            r, l = 2 * step - 1, 2 * step
            ag_copy[t, r] = send(ag.at[t, src_r], ag.at[t, r], asend.at[t, r], arecv.at[t, r], z_right)
            ag_copy[t, l] = send(ag.at[t, src_l], ag.at[t, l], asend.at[t, l], arecv.at[t, l], z_left)
            if t == 0:
                ag_copy[2, r] = send(ai.at[src_r], ai.at[r], isend.at[r], irecv.at[r], z_right)
                ag_copy[2, l] = send(ai.at[src_l], ai.at[l], isend.at[l], irecv.at[l], z_left)
        else:
            ag_copy[t, 7] = send(
                ag.at[t, 5, :, pl.ds(0, HD)], ag.at[t, 7, :, pl.ds(0, HD)], asend.at[t, 7], arecv.at[t, 7], z_right
            )
            ag_copy[t, 0] = send(
                ag.at[t, 6, :, pl.ds(HD, HD)], ag.at[t, 7, :, pl.ds(HD, HD)], asend.at[t, 0], arecv.at[t, 0], z_left
            )
            if t == 0:
                ag_copy[2, 7] = send(ai.at[5], ai.at[7], isend.at[7], irecv.at[7], z_right)

    seen = set()

    def once(t, s):
        if (t, s) not in seen:
            seen.add((t, s))
            ag_copy[t, s].wait_recv()

    def ag_wait(t, slots):
        for s in slots:
            once(t, s)
            if s == 7:
                once(t, 0)
            once(2, s)

    def gather(t, step):
        if step == 1:
            if t not in loaded:
                loads[2 + t].wait()
                loaded.add(t)
        else:
            ag_wait(t, (2 * step - 3, 2 * step - 2))
        ag_step(t, step)

    cached = set()

    def place_rows(place_row, weight_row):
        want = lax.broadcasted_iota(jnp.int32, (C, 128), 0).astype(F32)
        return jnp.where(place_row == want, weight_row, 0.0)

    def chooser(slot):
        if slot not in cached:
            cached.add(slot)
            table = ai[slot, z]
            for r in range(NY):
                yy = (y + r) % NY
                chooser_rows[slot, r * C : (r + 1) * C, :] = place_rows(line_of(table, yy), line_of(table, yy + 4))
        weights = chooser_rows[slot]
        return (weights > 0.0).astype(F32), weights

    y_copy = {}

    def rows(slot, r):
        return pl.ds(slot * 64 + r * C, C)

    def y_dst(t, slot, r):
        return xg.at[t, rows(slot, r)] if t < 2 else rback.at[t - 2, slot, r - 1]

    def y_src(t, slot, r):
        return sb.at[t, slot, r - 1] if t < 2 else eo.at[t - 2, rows(slot, r)]

    def crosses(t, slot):
        return t < 2 or slot >= 5

    def relay_side(t, slot):
        return y_right if (slot + (t if slot == 7 and t >= 2 else 0)) % 2 == 0 else y_left

    def y_send(t, slot):
        y_copy[t, slot, 0] = send(
            y_src(t, slot, 1), y_dst(t, slot, 3), ysend.at[t, slot, 0], yrecv.at[t, slot, 0], y_right
        )
        y_copy[t, slot, 1] = send(
            y_src(t, slot, 3), y_dst(t, slot, 1), ysend.at[t, slot, 1], yrecv.at[t, slot, 1], y_left
        )
        if crosses(t, slot):
            y_copy[t, slot, 2] = send(
                y_src(t, slot, 2), relay.at[t, slot], ysend.at[t, slot, 2], yrecv.at[t, slot, 2], relay_side(t, slot)
            )

    def y_relay(t, slot):
        y_copy[t, slot, 2].wait_recv()
        y_copy[t, slot, 3] = send(
            relay.at[t, slot], y_dst(t, slot, 2), ysend.at[t, slot, 3], yrecv.at[t, slot, 3], relay_side(t, slot)
        )

    def y_wait(t, *slots):
        for slot in slots:
            for i in (0, 1, 3):
                if i < 3 or crosses(t, slot):
                    y_copy[t, slot, i].wait_recv()

    def choose(t, slot):
        if slot > 0:
            ag_wait(t, (slot,))
        elif t not in loaded:
            loads[2 + t].wait()
            loaded.add(t)
        pick, weights = chooser(slot)
        chosen = dot(pick[:, :T].astype(BF), ag[t, slot])
        if t == 1:
            chosen = chosen * jnp.sum(weights, axis=1, keepdims=True)
        chosen = chosen.astype(BF)
        xg[t, rows(slot, 0), :] = chosen[0:C, :]
        for r in range(1, NY):
            sb[t, slot, r - 1] = chosen[r * C : (r + 1) * C, :]
        y_send(t, slot)

    down_ready = []

    def forward(c):
        y_wait(0, 2 * c, 2 * c + 1)
        if c == 0:
            loads[4].wait()
            loads[5].wait()
        band = pl.ds(c * 128, 128)

        @pl.loop(0, F // 256)
        def _(n):
            cols = pl.ds(pl.multiple_of(n * 256, 256), 256)
            g = dot(xg[0, band, :], wg[:, cols])
            u = dot(xg[0, band, :], wu[:, cols])
            gp[band, cols] = g
            up[band, cols] = u
            hid[band, cols] = (g * jax.nn.sigmoid(g) * u).astype(BF)

    def down(c):
        if not down_ready:
            loads[6].wait()
            down_ready.append(c)
        band = pl.ds(c * 128, 128)

        @pl.loop(0, D // 256)
        def _(n):
            cols = pl.ds(pl.multiple_of(n * 256, 256), 256)
            eo[0, band, cols] = dot(hid[band, :], wd[:, cols]).astype(BF)

    def backward(c):
        y_wait(1, 2 * c, 2 * c + 1)
        if not down_ready:
            loads[6].wait()
            down_ready.append(c)
        band = pl.ds(c * 128, 128)

        @pl.loop(0, F // 256)
        def _(n):
            cols = pl.ds(pl.multiple_of(n * 256, 256), 256)
            hg = dot_cols(xg[1, band, :], wd[cols, :])
            g = gp[band, cols]
            s = jax.nn.sigmoid(g)
            gg[band, cols] = (hg * up[band, cols] * s * (1.0 + g * (1.0 - s))).astype(BF)
            ug[band, cols] = (hg * g * s).astype(BF)

    def row_grad(c):
        band = pl.ds(c * 128, 128)

        @pl.loop(0, D // 256)
        def _(n):
            cols = pl.ds(pl.multiple_of(n * 256, 256), 256)
            eo[1, band, cols] = (dot_cols(gg[band, :], wg[cols, :]) + dot_cols(ug[band, :], wu[cols, :])).astype(BF)

    z_copy = {}

    def weigh(t, weights, got):
        if t == 1:
            return dot_rows((weights > 0.0).astype(F32)[:, :T].astype(BF), got)
        high = weights.astype(BF)
        low = (weights - high.astype(F32)).astype(BF)
        return dot_rows(high[:, :T], got) + dot_rows(low[:, :T], got)

    def combine(t, slot):
        weights = chooser(slot)[1]
        if crosses(2 + t, slot):
            got = [eo[t, rows(slot, 0), :], rback[t, slot, 0], rback[t, slot, 1], rback[t, slot, 2]]
        else:
            got = [eo[t, rows(slot, 0), :], rback[t, slot, 0], rback[t, slot, 2]]
            weights = jnp.concatenate([weights[0 : 2 * C], weights[3 * C : 4 * C]], axis=0)
        return weigh(t, weights, jnp.concatenate(got, axis=0))

    d_copy, far_copy = {}, {}

    def z_return(t, slot):
        device = (z_left, z_right, z_left2, z_right2)[slot - 1]
        d_copy[t, slot] = send(
            eo.at[t, rows(slot, 2)], rback.at[t, slot, 1], dsend.at[t, slot], drecv.at[t, slot], device
        )

    def far_first():
        far_copy[0] = send(far_send, far_relay, fsend.at[0], frecv.at[0], y_right)

    def far_second():
        far_copy[0].wait_recv()
        far_copy[1] = send(far_relay, far_info, fsend.at[1], frecv.at[1], y_right)

    def dense_sum(t):
        if t not in settled:
            settle(t)
        if 9 not in seen:
            seen.add(9)
            far_copy[1].wait_recv()
        for slot in range(1, 5):
            d_copy[t, slot].wait_recv()
        far = far_info[...]
        weights = jnp.concatenate([place_rows(far[2 * i : 2 * i + 1], far[2 * i + 1 : 2 * i + 2]) for i in range(5)], axis=0)
        got = [eo[t, rows(0, 2), :]] + [rback[t, slot, 1] for slot in range(1, 5)]
        ag[t, 0] = weigh(t, weights, jnp.concatenate(got, axis=0)).astype(BF)
        for i, device in ((0, y_right), (1, y_left)):
            cols = pl.ds(i * HD, HD)
            d_copy[t, 5 + i] = send(
                ag.at[t, 0, :, cols], drelay.at[t, :, cols],
                dsend.at[t, (0, 5)[i]], drecv.at[t, (0, 5)[i]], device,
            )

    def dense_relay(t):
        for i, device in ((0, y_right), (1, y_left)):
            cols = pl.ds(i * HD, HD)
            d_copy[t, 5 + i].wait_recv()
            d_copy[t, 7 + i] = send(
                drelay.at[t, :, cols], dland.at[t, :, cols], dsend.at[t, 6 + i], drecv.at[t, 6 + i], device
            )

    settled = set()

    def settle(t):
        settled.add(t)
        for key, copy in ag_copy.items():
            if key[0] == t:
                copy.wait_send()

    def z_step(t, slot):
        y_wait(t + 2, slot)
        total = combine(t, slot)
        if slot == 7:
            if t not in settled:
                settle(t)
            ag[t, 7] = total.astype(BF)
            z_copy[t, 0] = send(
                ag.at[t, 7, :, pl.ds(0, HD)], zrecv.at[t, 0, :, pl.ds(0, HD)],
                zsend.at[t, 0], zrecv_sem.at[t, 0], z_left,
            )
            z_copy[t, 4] = send(
                ag.at[t, 7, :, pl.ds(HD, HD)], zrecv.at[t, 0, :, pl.ds(HD, HD)],
                zsend.at[t, 4], zrecv_sem.at[t, 4], z_right,
            )
        elif slot > 0:
            leftward = slot % 2 == 1
            step = 3 - (slot - 1) // 2
            k = step if leftward else 4 + step
            z_copy[t, k - 1].wait_recv()
            if step == 1:
                half = pl.ds(0, HD) if leftward else pl.ds(HD, HD)
                lo = 0 if leftward else HD
                ag[t, slot] = total.astype(BF)
                ag[t, slot, :, half] = (total[:, lo : lo + HD] + zrecv[t, 0, :, half].astype(F32)).astype(BF)
            else:
                ag[t, slot] = (total + zrecv[t, k - 1].astype(F32)).astype(BF)
            z_copy[t, k] = send(
                ag.at[t, slot], zrecv.at[t, k], zsend.at[t, k], zrecv_sem.at[t, k], z_left if leftward else z_right
            )
        else:
            z_copy[t, 3].wait_recv()
            z_copy[t, 7].wait_recv()
            d_copy[t, 7].wait_recv()
            d_copy[t, 8].wait_recv()
            total = total + dland[t].astype(F32)
            out = layer_out if t == 0 else input_grad
            out[...] = (total + zrecv[t, 3].astype(F32) + zrecv[t, 7].astype(F32)).astype(BF)

    parts = (wd, pg, pu)
    outs = (down_out, gate_out, up_out)
    deep = (F // 8, D // 8, D // 8)
    wide = (D, F, F)
    cr_of = (cr_d.at[0], cr_a.at[0], cr_a.at[1])
    xh_of = (xh_d.at[0], xh_a.at[0], xh_a.at[1])
    xf_of = (xf_d.at[0], xf_a.at[0], xf_a.at[1])
    core_copy, x_copy = {}, {}

    def band_of(w, k, c):
        return pl.multiple_of(((x + k) % NX * 2 + c) * deep[w], 32)

    def core_send(w, k):
        block = pl.ds(band_of(w, k, 1 - core), deep[w])
        core_copy[w, k] = send(
            parts[w].at[block], cr_of[w].at[k], csend.at[w, k], crecv.at[w, k], other
        )

    def wgrad_tile(w, k, c):
        grad = gg if w == 1 else ug
        start = pl.multiple_of(((x + k) % NX * 2 + c) * 256, 256)
        parts[w][pl.ds(start, 256), :] = dot_rows(xg[0, :, pl.ds(start, 256)], grad[...]).astype(BF)

    owners = (2, 1, 3, 0)

    def wgrad(w, far, part):
        if w == 0:

            @pl.loop(2 * part, 2 * part + 2)
            def _(n):
                cols = pl.ds(pl.multiple_of(n * 256, 256), 256)
                wd[:, cols] = dot_rows(hid[...], xg[1, :, cols]).astype(BF)

            down_parts.add(part)
            if len(down_parts) == 4:
                for k in owners:
                    core_send(0, k)
        elif far:
            wgrad_tile(w, owners[part], 1 - core)
            core_send(w, owners[part])
        else:
            wgrad_tile(w, owners[part], core)

    down_parts = set()

    def add_block(w, k, extra, finish=None):
        first = band_of(w, k, core)
        size = 32

        @pl.loop(0, deep[w] // size)
        def _(i):
            mine = pl.ds(pl.multiple_of(first + i * size, size), size)
            at = pl.ds(pl.multiple_of(i * size, size), size)
            total = parts[w][mine, :].astype(F32) + cr_of[w][k, at, :].astype(F32)
            for ref in extra:
                total = total + ref[at, :].astype(F32)
            if finish is None:
                parts[w][mine, :] = total.astype(BF)
            else:
                finish[at, :] = total

    def x_first(w):
        core_copy[w, 2].wait_recv()
        add_block(w, 2, ())
        half = wide[w] // 2
        block = pl.ds(band_of(w, 2, core), deep[w])
        x_copy[w, 0] = send(
            parts[w].at[block, pl.ds(0, half)], xh_of[w].at[0], xsend.at[w, 0], xrecv.at[w, 0], x_right
        )
        x_copy[w, 1] = send(
            parts[w].at[block, pl.ds(half, half)], xh_of[w].at[1], xsend.at[w, 1], xrecv.at[w, 1], x_left
        )

    def x_second(w, i):
        half = wide[w] // 2
        k = (1, 3)[i]
        core_copy[w, k].wait_recv()
        add_block(w, k, ())
        x_copy[w, i].wait_recv()
        first = band_of(w, k, core)

        @pl.loop(0, deep[w] // 32)
        def _(j):
            mine = pl.ds(pl.multiple_of(first + j * 32, 32), 32)
            at = pl.ds(pl.multiple_of(j * 32, 32), 32)
            cols = pl.ds(i * half, half)
            parts[w][mine, cols] = (
                parts[w][mine, cols].astype(F32) + xh_of[w][i, at, :].astype(F32)
            ).astype(BF)

        x_copy[w, 2 + i] = send(
            parts[w].at[pl.ds(first, deep[w])], xf_of[w].at[i], xsend.at[w, 2 + i], xrecv.at[w, 2 + i],
            x_right if i == 0 else x_left,
        )

    def x_last(w):
        core_copy[w, 0].wait_recv()
        x_copy[w, 2].wait_recv()
        x_copy[w, 3].wait_recv()
        add_block(w, 0, (xf_of[w].at[0], xf_of[w].at[1]), outs[w])

    for step in (
        (gather, 0, 1), (far_first,), (gather, 1, 1), (choose, 0, 0), (choose, 1, 0), (gather, 0, 2), (choose, 0, 2),
        (y_relay, 0, 0), (choose, 0, 1), (choose, 1, 1), (gather, 1, 2), (far_second,), (y_relay, 0, 1),
        (choose, 1, 2), (choose, 0, 3), (gather, 0, 3), (y_relay, 1, 1), (y_relay, 1, 0), (choose, 0, 4),
        (forward, 0), (down, 0), (y_relay, 0, 2), (y_relay, 0, 3), (gather, 1, 3), (choose, 1, 3), (backward, 0),
        (choose, 0, 5), (choose, 0, 6), (gather, 0, 4), (y_relay, 1, 2), (y_relay, 0, 4), (gather, 1, 4),
        (forward, 1), (y_relay, 1, 3), (choose, 0, 7), (row_grad, 0), (choose, 1, 7), (y_relay, 0, 5),
        (choose, 1, 6), (down, 1), (y_relay, 0, 6), (backward, 1), (z_return, 0, 2), (y_relay, 0, 7), (row_grad, 1),
        (choose, 1, 5), (y_relay, 1, 7), (choose, 1, 4), (forward, 2), (z_return, 0, 3), (y_relay, 1, 6),
        (forward, 3), (down, 2), (z_return, 1, 2), (y_relay, 1, 5), (down, 3), (y_relay, 1, 4), (y_send, 2, 7),
        (z_return, 1, 1), (backward, 3), (row_grad, 3), (y_send, 3, 7), (z_return, 0, 1), (backward, 2),
        (z_return, 1, 3), (wgrad, 2, 1, 0), (wgrad, 1, 1, 0), (wgrad, 2, 0, 0), (y_relay, 2, 7), (y_send, 3, 6),
        (row_grad, 2), (y_send, 2, 6), (y_relay, 3, 7), (y_send, 3, 5), (wgrad, 2, 0, 1), (x_first, 2),
        (y_send, 2, 5), (wgrad, 2, 1, 2), (z_return, 0, 4), (wgrad, 2, 0, 2), (wgrad, 1, 0, 0), (z_step, 0, 7),
        (wgrad, 2, 1, 1), (x_first, 1), (wgrad, 0, 1, 1), (wgrad, 0, 1, 0), (wgrad, 1, 1, 1), (y_relay, 3, 5),
        (z_step, 1, 7), (y_relay, 3, 6), (y_relay, 2, 6), (x_second, 2, 0), (x_second, 2, 1), (y_send, 3, 3),
        (z_return, 1, 4), (wgrad, 0, 1, 2), (y_relay, 2, 5), (wgrad, 1, 1, 2), (z_step, 1, 5), (y_send, 3, 1),
        (y_send, 3, 4), (y_send, 2, 2), (z_step, 1, 6), (wgrad, 0, 1, 3), (z_step, 0, 6), (y_send, 2, 4),
        (y_send, 2, 3), (z_step, 0, 5), (x_first, 0), (y_send, 3, 2), (wgrad, 1, 0, 2), (wgrad, 1, 0, 1),
        (y_send, 3, 0), (x_second, 1, 0), (z_step, 1, 3), (z_step, 1, 4), (x_second, 1, 1), (y_send, 2, 1),
        (z_step, 0, 4), (dense_sum, 1), (z_step, 0, 3), (x_second, 0, 0), (y_send, 2, 0), (z_step, 1, 2),
        (x_second, 0, 1), (wgrad, 2, 1, 3), (z_step, 1, 1), (dense_sum, 0), (z_step, 0, 2), (dense_relay, 1),
        (z_step, 0, 1), (wgrad, 1, 1, 3), (dense_relay, 0), (wgrad, 2, 0, 3), (wgrad, 1, 0, 3), (z_step, 1, 0),
        (x_last, 2), (x_last, 1), (z_step, 0, 0), (x_last, 0),
    ):
        step[0](*step[1:])

    early = [id(copy) for key, copy in ag_copy.items() if key[0] < 2]
    for copy in started:
        if id(copy) not in early:
            copy.wait_send()


def store(*refs):
    copies = [pltpu.make_async_copy(refs[i], refs[5 + i], refs[10].at[i]) for i in range(5)]
    for copy in copies:
        copy.start()
    for copy in copies:
        copy.wait()


def shards(tokens, expert_ids, gate_probs, out_cot, w_gate, w_up, w_down):
    vmem = pl.BlockSpec(memory_space=pltpu.VMEM)
    hbm = pl.BlockSpec(memory_space=pl.ANY)
    dma = pltpu.SemaphoreType.DMA
    V = pltpu.VMEM
    results = pl.pallas_call(
        kernel,
        out_shape=(
            V((T, D), BF),
            V((T, D), BF),
            V((D // 8, F), F32),
            V((D // 8, F), F32),
            V((F // 8, D), F32),
        ),
        in_specs=[hbm] * 7,
        out_specs=(vmem,) * 5,
        scratch_shapes=[
            V((8, T), jnp.int32),
            V((8, T), F32),
            V((NZ, NY * C, 128), F32),
            V((16, 128), F32),
            V((16, 128), F32),
            V((16, 128), F32),
            V((2, T, D), BF),
            V((2, T, D), BF),
            V((2, NZ, T, D), BF),
            V((NZ, NZ, 8, 128), F32),
            V((2, NZ, 3, C, D), BF),
            V((2, ROWS, D), BF),
            V((2, ROWS, D), BF),
            V((2, NZ, 3, C, D), BF),
            V((4, NZ, C, D), BF),
            V((D, F), BF),
            V((D, F), BF),
            V((F, D), BF),
            V((ROWS, F), F32),
            V((ROWS, F), F32),
            V((ROWS, F), BF),
            V((ROWS, F), BF),
            V((ROWS, F), BF),
            V((2, NZ, T, D), BF),
            V((D, F), BF),
            V((D, F), BF),
            V((2, NX, D // 8, F), BF),
            V((1, NX, F // 8, D), BF),
            V((2, 2, D // 8, F // 2), BF),
            V((1, 2, F // 8, D // 2), BF),
            V((2, 2, D // 8, F), BF),
            V((1, 2, F // 8, D), BF),
            dma((7,)),
            dma((4, NZ, 4)),
            dma((4, NZ, 4)),
            dma((2, NZ)),
            dma((2, NZ)),
            dma((NZ,)),
            dma((NZ,)),
            dma((2, 8)),
            dma((2, 8)),
            dma((3, NX)),
            dma((3, NX)),
            dma((3, 4)),
            dma((3, 4)),
            dma((2,)),
            dma((2,)),
            dma((2, 8)),
            dma((2, 8)),
        ],
        compiler_params=pltpu.CompilerParams(
            collective_id=0, has_side_effects=True, vmem_limit_bytes=63_900_000
        ),
        name="expert_layer",
    )(expert_ids.T, gate_probs.T, tokens, out_cot, w_gate[0], w_up[0], w_down[0])
    layer_out, input_grad, gate, up, down = pl.pallas_call(
        store,
        out_shape=tuple(jax.ShapeDtypeStruct(r.shape, r.dtype) for r in results),
        in_specs=[hbm] * 5,
        out_specs=(hbm,) * 5,
        scratch_shapes=[dma((5,))],
        compiler_params=pltpu.CompilerParams(vmem_limit_bytes=1 << 20),
        name="store",
    )(*results)
    return (layer_out, input_grad, gate[None], up[None], down[None])


def solution(mesh):
    placed = (
        P(("dp", "expert"), None),
        P(("dp", "expert"), None),
        P(("dp", "expert"), None),
        P(("dp", "expert"), None),
        P("expert", None, None),
        P("expert", None, None),
        P("expert", None, None),
    )
    return jax.shard_map(
        shards,
        mesh=mesh,
        in_specs=placed,
        out_specs=(
            P(("dp", "expert"), None),
            P(("dp", "expert"), None),
            P("expert", "dp", None),
            P("expert", "dp", None),
            P("expert", "dp", None),
        ),
        check_vma=False,
    )
```

```python
import jax
import jax.numpy as jnp
from jax import lax
from jax.experimental import pallas as pl
from jax.experimental.pallas import tpu as pltpu
from jax.sharding import PartitionSpec as P

MESH = pl.DeviceIdType.MESH
BF = jnp.bfloat16
F32 = jnp.float32
NZ, NY, NX = 8, 4, 4
T, C, D, F = 48, 16, 2048, 768
EXPERTS = NZ * NY
ROWS = NZ * NY * C
HD = D // 2
BACK = (7, 5, 6, 3, 4, 1, 2, 0)


def dot(a, b):
    return jnp.dot(a, b, preferred_element_type=F32)


def dot_cols(a, b):
    return lax.dot_general(a, b, (((1,), (1,)), ((), ())), preferred_element_type=F32)


def dot_rows(a, b):
    return lax.dot_general(a, b, (((0,), (0,)), ((), ())), preferred_element_type=F32)


def kernel(
    ids_hbm, probs_hbm, tok_hbm, cot_hbm, wg_hbm, wu_hbm, wd_hbm,
    layer_out, input_grad, gate_out, up_out, down_out,
    ids, probs, chooser_rows, far_send, far_relay, far_info, far_rows, prelay, pland, drelay, dland, ag, ai, sb, xg, eo, rback, relay, wg, wu, wd, gp, up, hid, gg, ug,
    zrecv, pg, pu, cr_a, cr_d, xh_a, xh_d, xf_a, xf_d,
    loc, ysend, yrecv, asend, arecv, isend, irecv, zsend, zrecv_sem, csend, crecv, xsend, xrecv, fsend, frecv,
    dsend, drecv, psend, precv,
):
    ex = lax.axis_index("expert")
    dp = lax.axis_index("dp")
    z, y = ex // NY, ex % NY
    x, core = dp // 2, dp % 2
    z_right = {"expert": (z + 1) % NZ * NY + y}
    z_left = {"expert": (z + NZ - 1) % NZ * NY + y}
    z_right2 = {"expert": (z + 2) % NZ * NY + y}
    z_left2 = {"expert": (z + NZ - 2) % NZ * NY + y}
    y_right = {"expert": z * NY + (y + 1) % NY}
    y_left = {"expert": z * NY + (y + NY - 1) % NY}
    x_right = {"dp": (x + 1) % NX * 2 + core}
    x_left = {"dp": (x + NX - 1) % NX * 2 + core}
    other = {"dp": x * 2 + 1 - core}

    def line_of(table, index):
        line = lax.broadcasted_iota(jnp.int32, (8, 128), 0)
        return jnp.sum(jnp.where(line == index, table, 0.0), axis=0, keepdims=True)

    started = []

    def send(src, dst, ssem, rsem, device):
        copy = pltpu.make_async_remote_copy(
            src_ref=src, dst_ref=dst, send_sem=ssem, recv_sem=rsem, device_id=device, device_id_type=MESH
        )
        copy.start()
        started.append(copy)
        return copy

    loads = {}
    for i, (src, dst) in enumerate(
        (
            (ids_hbm, ids), (probs_hbm, probs), (tok_hbm, ag.at[0, 0]), (cot_hbm, ag.at[1, 0]),
            (wg_hbm, wg), (wu_hbm, wu), (wd_hbm, wd),
        )
    ):
        loads[i] = pltpu.make_async_copy(src, dst, loc.at[i])
        loads[i].start()

    barrier = pltpu.get_barrier_semaphore()
    for device in (z_right, z_left, z_right2, z_left2, y_right, y_left, x_right, x_left, other):
        pl.semaphore_signal(barrier, inc=1, device_id=device, device_id_type=MESH)

    loads[0].wait()
    loads[1].wait()
    fill = jnp.full((8, 128 - T), -1, jnp.int32)
    chosen_ids = jnp.concatenate([ids[...], fill], axis=1)
    chosen_probs = jnp.concatenate([probs[...], fill.astype(F32)], axis=1)
    expert_row = lax.broadcasted_iota(jnp.int32, (EXPERTS, 128), 0)
    named = jnp.zeros((EXPERTS, 128), F32)
    weight = jnp.zeros((EXPERTS, 128), F32)
    for k in range(8):
        same = chosen_ids[k : k + 1, :] == expert_row
        named = jnp.where(same, 1.0, named)
        weight = jnp.where(same, chosen_probs[k : k + 1, :], weight)
    before = (
        lax.broadcasted_iota(jnp.int32, (128, 128), 0) < lax.broadcasted_iota(jnp.int32, (128, 128), 1)
    ).astype(F32).astype(BF)
    place = jnp.where(named > 0.0, dot(named.astype(BF), before), -1.0)
    for p in range(NZ):
        ai[0, p, 0:4, :] = place[4 * p : 4 * p + 4, :]
        ai[0, p, 4:8, :] = weight[4 * p : 4 * p + 4, :]

    for i, shift in enumerate((0, 1, NZ - 1, 2, NZ - 2)):
        table = ai[0, (z + shift) % NZ]
        far_send[2 * i : 2 * i + 1, :] = line_of(table, (y + 2) % NY)
        far_send[2 * i + 1 : 2 * i + 2, :] = line_of(table, (y + 2) % NY + 4)
    far_send[10:16, :] = jnp.zeros((6, 128), F32)

    pl.semaphore_wait(barrier, 9)

    loaded = set()

    def own_block(t):
        if t not in loaded:
            loads[2 + t].wait()
            loaded.add(t)


    ag_copy = {}

    def ag_step(t, step):
        if step < 4:
            src_r, src_l = (0, 0) if step == 1 else (2 * step - 3, 2 * step - 2)
            r, l = 2 * step - 1, 2 * step
            ag_copy[t, r] = send(ag.at[t, src_r], ag.at[t, r], asend.at[t, r], arecv.at[t, r], z_right)
            ag_copy[t, l] = send(ag.at[t, src_l], ag.at[t, l], asend.at[t, l], arecv.at[t, l], z_left)
            if t == 0:
                ag_copy[2, r] = send(ai.at[src_r], ai.at[r], isend.at[r], irecv.at[r], z_right)
                ag_copy[2, l] = send(ai.at[src_l], ai.at[l], isend.at[l], irecv.at[l], z_left)
        else:
            ag_copy[t, 7] = send(
                ag.at[t, 5, :, pl.ds(0, HD)], ag.at[t, 7, :, pl.ds(0, HD)], asend.at[t, 7], arecv.at[t, 7], z_right
            )
            ag_copy[t, 0] = send(
                ag.at[t, 6, :, pl.ds(HD, HD)], ag.at[t, 7, :, pl.ds(HD, HD)], asend.at[t, 0], arecv.at[t, 0], z_left
            )
            if t == 0:
                ag_copy[2, 7] = send(ai.at[5], ai.at[7], isend.at[7], irecv.at[7], z_right)

    seen = set()

    def once(t, s):
        if (t, s) not in seen:
            seen.add((t, s))
            ag_copy[t, s].wait_recv()

    def ag_wait(t, slots):
        for s in slots:
            once(t, s)
            if s == 7:
                once(t, 0)
            once(2, s)

    def gather(t, step):
        if step == 1:
            own_block(t)
        else:
            ag_wait(t, (2 * step - 3, 2 * step - 2))
        ag_step(t, step)

    cached = set()

    def place_rows(place_row, weight_row):
        want = lax.broadcasted_iota(jnp.int32, (C, 128), 0).astype(F32)
        return jnp.where(place_row == want, weight_row, 0.0)

    def chooser(slot):
        if slot not in cached:
            cached.add(slot)
            table = ai[slot, z]
            for r in range(NY):
                yy = (y + r) % NY
                chooser_rows[slot, r * C : (r + 1) * C, :] = place_rows(line_of(table, yy), line_of(table, yy + 4))
        weights = chooser_rows[slot]
        if slot >= 5:
            return weights, (0, 1, 2, 3)
        return jnp.concatenate([weights[0 : 2 * C], weights[3 * C : 4 * C]], axis=0), (0, 1, 3)

    y_copy = {}

    def rows(slot, r):
        return pl.ds(slot * 64 + r * C, C)

    def y_dst(t, slot, r):
        return xg.at[t, rows(slot, r)] if t < 2 else rback.at[t - 2, slot, r - 1]

    def y_src(t, slot, r):
        return sb.at[t, slot, r - 1] if t < 2 else eo.at[t - 2, rows(slot, r)]

    def relay_side(t, slot):
        return y_right if (slot + (t if slot == 7 else 0)) % 2 == 0 else y_left

    def y_send(t, slot):
        y_copy[t, slot, 0] = send(
            y_src(t, slot, 1), y_dst(t, slot, 3), ysend.at[t, slot, 0], yrecv.at[t, slot, 0], y_right
        )
        y_copy[t, slot, 1] = send(
            y_src(t, slot, 3), y_dst(t, slot, 1), ysend.at[t, slot, 1], yrecv.at[t, slot, 1], y_left
        )
        if slot >= 5:
            y_copy[t, slot, 2] = send(
                y_src(t, slot, 2), relay.at[t, slot - 5], ysend.at[t, slot, 2], yrecv.at[t, slot, 2], relay_side(t, slot)
            )

    def y_relay(t, slot):
        y_copy[t, slot, 2].wait_recv()
        y_copy[t, slot, 3] = send(
            relay.at[t, slot - 5], y_dst(t, slot, 2), ysend.at[t, slot, 3], yrecv.at[t, slot, 3], relay_side(t, slot)
        )

    def y_wait(t, *slots):
        for slot in slots:
            for i in (0, 1, 3):
                if i < 3 or slot >= 5:
                    y_copy[t, slot, i].wait_recv()
            if t < 2 and 1 <= slot <= 4:
                p_copy[t, slot].wait_recv()

    def pick_rows(t, weights, block):
        chosen = dot((weights > 0.0).astype(F32)[:, :T].astype(BF), block)
        if t == 1:
            chosen = chosen * jnp.sum(weights, axis=1, keepdims=True)
        return chosen.astype(BF)

    def choose(t, slot):
        if slot > 0:
            ag_wait(t, (slot,))
        else:
            own_block(t)
        weights, groups = chooser(slot)
        chosen = pick_rows(t, weights, ag[t, slot])
        for i, r in enumerate(groups):
            if r == 0:
                xg[t, rows(slot, 0), :] = chosen[0:C, :]
            else:
                sb[t, slot, r - 1] = chosen[i * C : (i + 1) * C, :]
        y_send(t, slot)

    down_ready, up_ready = [], []

    def forward(c):
        y_wait(0, 2 * c, 2 * c + 1)
        if not up_ready:
            loads[4].wait()
            loads[5].wait()
            up_ready.append(c)
        band = pl.ds(c * 128, 128)

        @pl.loop(0, F // 256)
        def _(n):
            cols = pl.ds(pl.multiple_of(n * 256, 256), 256)
            g = dot(xg[0, band, :], wg[:, cols])
            u = dot(xg[0, band, :], wu[:, cols])
            gp[band, cols] = g
            up[band, cols] = u
            hid[band, cols] = (g * jax.nn.sigmoid(g) * u).astype(BF)

    def down(c):
        if not down_ready:
            loads[6].wait()
            down_ready.append(c)
        band = pl.ds(c * 128, 128)

        @pl.loop(0, D // 256)
        def _(n):
            cols = pl.ds(pl.multiple_of(n * 256, 256), 256)
            eo[0, band, cols] = dot(hid[band, :], wd[:, cols]).astype(BF)

    def backward(c):
        y_wait(1, 2 * c, 2 * c + 1)
        if not down_ready:
            loads[6].wait()
            down_ready.append(c)
        band = pl.ds(c * 128, 128)

        @pl.loop(0, F // 256)
        def _(n):
            cols = pl.ds(pl.multiple_of(n * 256, 256), 256)
            hg = dot_cols(xg[1, band, :], wd[cols, :])
            g = gp[band, cols]
            s = jax.nn.sigmoid(g)
            gg[band, cols] = (hg * up[band, cols] * s * (1.0 + g * (1.0 - s))).astype(BF)
            ug[band, cols] = (hg * g * s).astype(BF)

    def row_grad(c):
        band = pl.ds(c * 128, 128)

        @pl.loop(0, D // 256)
        def _(n):
            cols = pl.ds(pl.multiple_of(n * 256, 256), 256)
            eo[1, band, cols] = (dot_cols(gg[band, :], wg[cols, :]) + dot_cols(ug[band, :], wu[cols, :])).astype(BF)

    z_copy = {}

    def weigh(t, weights, got):
        if t == 1:
            return dot_rows((weights > 0.0).astype(F32)[:, :T].astype(BF), got)
        high = weights.astype(BF)
        low = (weights - high.astype(F32)).astype(BF)
        return dot_rows(high[:, :T], got) + dot_rows(low[:, :T], got)

    def combine(t, slot):
        weights, groups = chooser(slot)
        got = [eo[t, rows(slot, 0), :]] + [rback[t, slot, r - 1] for r in groups[1:]]
        return weigh(t, weights, jnp.concatenate(got, axis=0))

    d_copy, far_copy = {}, {}

    def z_return(t, slot):
        device = (z_left, z_right, z_left2, z_right2)[slot - 1]
        d_copy[t, slot] = send(
            eo.at[t, rows(slot, 2)], rback.at[t, slot, 1], dsend.at[t, slot], drecv.at[t, slot], device
        )

    def far_first():
        far_copy[0] = send(far_send, far_relay, fsend.at[0], frecv.at[0], y_right)

    def far_second():
        far_copy[0].wait_recv()
        far_copy[1] = send(far_relay, far_info, fsend.at[1], frecv.at[1], y_right)

    p_copy = {}

    def dense_first(t):
        own_block(t)
        if t == 0:
            far_first()
        for i, device in ((0, y_right), (1, y_left)):
            cols = pl.ds(i * HD, HD)
            p_copy[t, 5 + i] = send(
                ag.at[t, 0, :, cols], prelay.at[t, :, cols],
                psend.at[t, (0, 5)[i]], precv.at[t, (0, 5)[i]], device,
            )

    def dense_pass(t):
        if t == 0:
            far_second()
        for i, device in ((0, y_right), (1, y_left)):
            cols = pl.ds(i * HD, HD)
            p_copy[t, 5 + i].wait_recv()
            p_copy[t, 7 + i] = send(
                prelay.at[t, :, cols], pland.at[t, :, cols], psend.at[t, 6 + i], precv.at[t, 6 + i], device
            )

    def far_ready():
        if 9 not in seen:
            seen.add(9)
            far_copy[1].wait_recv()
            far = far_info[...]
            for i in range(5):
                far_rows[i * C : (i + 1) * C, :] = place_rows(far[2 * i : 2 * i + 1], far[2 * i + 1 : 2 * i + 2])
        return far_rows[...]

    def dense_choose(t):
        p_copy[t, 7].wait_recv()
        p_copy[t, 8].wait_recv()
        chosen = pick_rows(t, far_ready(), pland[t])
        xg[t, rows(0, 2), :] = chosen[0:C, :]
        for slot in (3, 4, 1, 2):
            sb[t, slot, 1] = chosen[slot * C : (slot + 1) * C, :]
            device = (z_right, z_left, z_right2, z_left2)[slot - 1]
            p_copy[t, slot] = send(
                sb.at[t, slot, 1], xg.at[t, rows(slot, 2)], psend.at[t, slot], precv.at[t, slot], device
            )

    def dense_sum(t):
        if t not in settled:
            settle(t)
        weights = far_ready()
        for slot in range(1, 5):
            d_copy[t, slot].wait_recv()
        got = [eo[t, rows(0, 2), :]] + [rback[t, slot, 1] for slot in range(1, 5)]
        ag[t, 0] = weigh(t, weights, jnp.concatenate(got, axis=0)).astype(BF)
        for i, device in ((0, y_right), (1, y_left)):
            cols = pl.ds(i * HD, HD)
            d_copy[t, 5 + i] = send(
                ag.at[t, 0, :, cols], drelay.at[t, :, cols],
                dsend.at[t, (0, 5)[i]], drecv.at[t, (0, 5)[i]], device,
            )

    def dense_relay(t):
        for i, device in ((0, y_right), (1, y_left)):
            cols = pl.ds(i * HD, HD)
            d_copy[t, 5 + i].wait_recv()
            d_copy[t, 7 + i] = send(
                drelay.at[t, :, cols], dland.at[t, :, cols], dsend.at[t, 6 + i], drecv.at[t, 6 + i], device
            )

    settled, finished = set(), []

    def settle(t):
        settled.add(t)
        for key, copy in ag_copy.items():
            if key[0] == t:
                copy.wait_send()
                finished.append(id(copy))
        for k in (5, 6):
            p_copy[t, k].wait_send()
            finished.append(id(p_copy[t, k]))

    def z_step(t, slot):
        y_wait(t + 2, slot)
        total = combine(t, slot)
        if slot == 7:
            if t not in settled:
                settle(t)
            ag[t, 7] = total.astype(BF)
            z_copy[t, 0] = send(
                ag.at[t, 7, :, pl.ds(0, HD)], zrecv.at[t, 0, :, pl.ds(0, HD)],
                zsend.at[t, 0], zrecv_sem.at[t, 0], z_left,
            )
            z_copy[t, 4] = send(
                ag.at[t, 7, :, pl.ds(HD, HD)], zrecv.at[t, 0, :, pl.ds(HD, HD)],
                zsend.at[t, 4], zrecv_sem.at[t, 4], z_right,
            )
        elif slot > 0:
            leftward = slot % 2 == 1
            step = 3 - (slot - 1) // 2
            k = step if leftward else 4 + step
            z_copy[t, k - 1].wait_recv()
            if step == 1:
                half = pl.ds(0, HD) if leftward else pl.ds(HD, HD)
                lo = 0 if leftward else HD
                ag[t, slot] = total.astype(BF)
                ag[t, slot, :, half] = (total[:, lo : lo + HD] + zrecv[t, 0, :, half].astype(F32)).astype(BF)
            else:
                ag[t, slot] = (total + zrecv[t, k - 1].astype(F32)).astype(BF)
            z_copy[t, k] = send(
                ag.at[t, slot], zrecv.at[t, k], zsend.at[t, k], zrecv_sem.at[t, k], z_left if leftward else z_right
            )
        else:
            z_copy[t, 3].wait_recv()
            z_copy[t, 7].wait_recv()
            d_copy[t, 7].wait_recv()
            d_copy[t, 8].wait_recv()
            total = total + dland[t].astype(F32)
            out = layer_out if t == 0 else input_grad
            out[...] = (total + zrecv[t, 3].astype(F32) + zrecv[t, 7].astype(F32)).astype(BF)

    parts = (wd, pg, pu)
    outs = (down_out, gate_out, up_out)
    deep = (F // 8, D // 8, D // 8)
    wide = (D, F, F)
    cr_of = (cr_d.at[0], cr_a.at[0], cr_a.at[1])
    xh_of = (xh_d.at[0], xh_a.at[0], xh_a.at[1])
    xf_of = (xf_d.at[0], xf_a.at[0], xf_a.at[1])
    core_copy, x_copy = {}, {}

    def band_of(w, k, c):
        return pl.multiple_of(((x + k) % NX * 2 + c) * deep[w], 32)

    def core_send(w, k):
        block = pl.ds(band_of(w, k, 1 - core), deep[w])
        core_copy[w, k] = send(
            parts[w].at[block], cr_of[w].at[k], csend.at[w, k], crecv.at[w, k], other
        )

    def wgrad_tile(w, k, c):
        grad = gg if w == 1 else ug
        start = pl.multiple_of(((x + k) % NX * 2 + c) * 256, 256)
        parts[w][pl.ds(start, 256), :] = dot_rows(xg[0, :, pl.ds(start, 256)], grad[...]).astype(BF)

    owners = (2, 1, 3, 0)

    def wgrad(w, far, part):
        if w == 0:

            @pl.loop(2 * part, 2 * part + 2)
            def _(n):
                cols = pl.ds(pl.multiple_of(n * 256, 256), 256)
                wd[:, cols] = dot_rows(hid[...], xg[1, :, cols]).astype(BF)

            down_parts.add(part)
            if len(down_parts) == 4:
                for k in owners:
                    core_send(0, k)
        elif far:
            wgrad_tile(w, owners[part], 1 - core)
            core_send(w, owners[part])
        else:
            wgrad_tile(w, owners[part], core)

    down_parts = set()

    def add_block(w, k, extra, finish=None):
        first = band_of(w, k, core)
        size = 32

        @pl.loop(0, deep[w] // size)
        def _(i):
            mine = pl.ds(pl.multiple_of(first + i * size, size), size)
            at = pl.ds(pl.multiple_of(i * size, size), size)
            total = parts[w][mine, :].astype(F32) + cr_of[w][k, at, :].astype(F32)
            for ref in extra:
                total = total + ref[at, :].astype(F32)
            if finish is None:
                parts[w][mine, :] = total.astype(BF)
            else:
                finish[at, :] = total

    def x_first(w):
        core_copy[w, 2].wait_recv()
        add_block(w, 2, ())
        half = wide[w] // 2
        block = pl.ds(band_of(w, 2, core), deep[w])
        x_copy[w, 0] = send(
            parts[w].at[block, pl.ds(0, half)], xh_of[w].at[0], xsend.at[w, 0], xrecv.at[w, 0], x_right
        )
        x_copy[w, 1] = send(
            parts[w].at[block, pl.ds(half, half)], xh_of[w].at[1], xsend.at[w, 1], xrecv.at[w, 1], x_left
        )

    def x_second(w, i):
        half = wide[w] // 2
        k = (1, 3)[i]
        core_copy[w, k].wait_recv()
        add_block(w, k, ())
        x_copy[w, i].wait_recv()
        first = band_of(w, k, core)

        @pl.loop(0, deep[w] // 32)
        def _(j):
            mine = pl.ds(pl.multiple_of(first + j * 32, 32), 32)
            at = pl.ds(pl.multiple_of(j * 32, 32), 32)
            cols = pl.ds(i * half, half)
            parts[w][mine, cols] = (
                parts[w][mine, cols].astype(F32) + xh_of[w][i, at, :].astype(F32)
            ).astype(BF)

        x_copy[w, 2 + i] = send(
            parts[w].at[pl.ds(first, deep[w])], xf_of[w].at[i], xsend.at[w, 2 + i], xrecv.at[w, 2 + i],
            x_right if i == 0 else x_left,
        )

    def x_last(w):
        core_copy[w, 0].wait_recv()
        x_copy[w, 2].wait_recv()
        x_copy[w, 3].wait_recv()
        add_block(w, 0, (xf_of[w].at[0], xf_of[w].at[1]), outs[w])

    for step in (
        (dense_first, 1), (gather, 0, 1), (dense_first, 0), (gather, 1, 1), (gather, 0, 2), (dense_pass, 1),
        (dense_pass, 0), (choose, 1, 2), (gather, 1, 2), (choose, 1, 1), (choose, 1, 0), (choose, 0, 0),
        (choose, 0, 4), (gather, 0, 3), (choose, 0, 1), (choose, 0, 2), (choose, 1, 4), (choose, 0, 3),
        (gather, 1, 3), (dense_choose, 0), (choose, 1, 3), (choose, 0, 6), (gather, 0, 4), (choose, 0, 5),
        (choose, 1, 5), (gather, 1, 4), (choose, 1, 6), (dense_choose, 1), (y_relay, 0, 5), (y_relay, 0, 6),
        (forward, 1), (y_relay, 1, 5), (forward, 0), (y_relay, 1, 6), (choose, 0, 7), (down, 1), (down, 0),
        (choose, 1, 7), (forward, 2), (down, 2), (z_return, 0, 2), (y_relay, 0, 7), (y_send, 2, 5), (backward, 2),
        (backward, 1), (y_relay, 1, 7), (backward, 0), (forward, 3), (down, 3), (y_send, 2, 7), (y_send, 2, 6),
        (z_return, 0, 3), (backward, 3), (wgrad, 2, 1, 0), (wgrad, 2, 0, 0), (row_grad, 3), (z_return, 0, 1),
        (z_return, 0, 4), (y_send, 3, 7), (row_grad, 2), (x_first, 2), (y_relay, 2, 7), (wgrad, 1, 1, 0),
        (wgrad, 2, 1, 1), (z_return, 1, 4), (y_send, 3, 6), (wgrad, 1, 0, 0), (wgrad, 2, 1, 2), (y_relay, 2, 5),
        (wgrad, 0, 1, 1), (row_grad, 1), (x_first, 1), (y_relay, 3, 7), (z_return, 1, 3), (y_send, 3, 5),
        (wgrad, 0, 1, 0), (z_step, 0, 7), (y_relay, 2, 6), (wgrad, 2, 0, 2), (wgrad, 2, 0, 1), (z_return, 1, 2),
        (y_relay, 3, 6), (x_second, 2, 0), (y_send, 2, 0), (x_second, 2, 1), (z_step, 1, 7), (wgrad, 1, 1, 2),
        (y_relay, 3, 5), (y_send, 3, 3), (wgrad, 1, 1, 1), (y_send, 2, 3), (z_step, 0, 5), (z_step, 0, 6),
        (wgrad, 0, 1, 2), (wgrad, 0, 1, 3), (wgrad, 1, 0, 1), (y_send, 3, 4), (z_step, 1, 5), (y_send, 2, 4),
        (wgrad, 1, 0, 2), (z_step, 1, 6), (y_send, 2, 1), (x_first, 0), (z_step, 0, 3), (x_second, 1, 0),
        (x_second, 1, 1), (y_send, 3, 2), (z_step, 0, 4), (row_grad, 0), (z_return, 1, 1), (y_send, 2, 2),
        (z_step, 1, 3), (z_step, 1, 4), (x_second, 0, 1), (y_send, 3, 1), (y_send, 3, 0), (dense_sum, 0),
        (z_step, 0, 2), (x_second, 0, 0), (z_step, 0, 1), (dense_sum, 1), (z_step, 1, 1), (wgrad, 2, 1, 3),
        (dense_relay, 0), (z_step, 1, 2), (wgrad, 1, 1, 3), (dense_relay, 1), (wgrad, 2, 0, 3), (z_step, 0, 0),
        (wgrad, 1, 0, 3), (x_last, 1), (x_last, 2), (z_step, 1, 0), (x_last, 0),
    ):
        step[0](*step[1:])

    for copy in started:
        if id(copy) not in finished:
            copy.wait_send()


def store(*refs):
    copies = [pltpu.make_async_copy(refs[i], refs[5 + i], refs[10].at[i]) for i in range(5)]
    for copy in copies:
        copy.start()
    for copy in copies:
        copy.wait()


def shards(tokens, expert_ids, gate_probs, out_cot, w_gate, w_up, w_down):
    vmem = pl.BlockSpec(memory_space=pltpu.VMEM)
    hbm = pl.BlockSpec(memory_space=pl.ANY)
    dma = pltpu.SemaphoreType.DMA
    V = pltpu.VMEM
    results = pl.pallas_call(
        kernel,
        out_shape=(
            V((T, D), BF),
            V((T, D), BF),
            V((D // 8, F), F32),
            V((D // 8, F), F32),
            V((F // 8, D), F32),
        ),
        in_specs=[hbm] * 7,
        out_specs=(vmem,) * 5,
        scratch_shapes=[
            V((8, T), jnp.int32),
            V((8, T), F32),
            V((NZ, NY * C, 128), F32),
            V((16, 128), F32),
            V((16, 128), F32),
            V((16, 128), F32),
            V((5 * C, 128), F32),
            V((2, T, D), BF),
            V((2, T, D), BF),
            V((2, T, D), BF),
            V((2, T, D), BF),
            V((2, NZ, T, D), BF),
            V((NZ, NZ, 8, 128), F32),
            V((2, NZ, 3, C, D), BF),
            V((2, ROWS, D), BF),
            V((2, ROWS, D), BF),
            V((2, NZ, 3, C, D), BF),
            V((4, 3, C, D), BF),
            V((D, F), BF),
            V((D, F), BF),
            V((F, D), BF),
            V((ROWS, F), F32),
            V((ROWS, F), F32),
            V((ROWS, F), BF),
            V((ROWS, F), BF),
            V((ROWS, F), BF),
            V((2, NZ, T, D), BF),
            V((D, F), BF),
            V((D, F), BF),
            V((2, NX, D // 8, F), BF),
            V((1, NX, F // 8, D), BF),
            V((2, 2, D // 8, F // 2), BF),
            V((1, 2, F // 8, D // 2), BF),
            V((2, 2, D // 8, F), BF),
            V((1, 2, F // 8, D), BF),
            dma((7,)),
            dma((4, NZ, 4)),
            dma((4, NZ, 4)),
            dma((2, NZ)),
            dma((2, NZ)),
            dma((NZ,)),
            dma((NZ,)),
            dma((2, 8)),
            dma((2, 8)),
            dma((3, NX)),
            dma((3, NX)),
            dma((3, 4)),
            dma((3, 4)),
            dma((2,)),
            dma((2,)),
            dma((2, 8)),
            dma((2, 8)),
            dma((2, 8)),
            dma((2, 8)),
        ],
        compiler_params=pltpu.CompilerParams(
            collective_id=0, has_side_effects=True, vmem_limit_bytes=63_900_000
        ),
        name="expert_layer",
    )(expert_ids.T, gate_probs.T, tokens, out_cot, w_gate[0], w_up[0], w_down[0])
    layer_out, input_grad, gate, up, down = pl.pallas_call(
        store,
        out_shape=tuple(jax.ShapeDtypeStruct(r.shape, r.dtype) for r in results),
        in_specs=[hbm] * 5,
        out_specs=(hbm,) * 5,
        scratch_shapes=[dma((5,))],
        compiler_params=pltpu.CompilerParams(vmem_limit_bytes=1 << 20),
        name="store",
    )(*results)
    return (layer_out, input_grad, gate[None], up[None], down[None])


def solution(mesh):
    placed = (
        P(("dp", "expert"), None),
        P(("dp", "expert"), None),
        P(("dp", "expert"), None),
        P(("dp", "expert"), None),
        P("expert", None, None),
        P("expert", None, None),
        P("expert", None, None),
    )
    return jax.shard_map(
        shards,
        mesh=mesh,
        in_specs=placed,
        out_specs=(
            P(("dp", "expert"), None),
            P(("dp", "expert"), None),
            P("expert", "dp", None),
            P("expert", "dp", None),
            P("expert", "dp", None),
        ),
        check_vma=False,
    )
```
